32 devices in a mesh: shard: 4 (over z), ctx: 4 (over y, x), tp: 2 (over core).
Axes of the slice: x: 2, y: 2, z: 4, core: 2. Of those that a mesh axis runs over, the one named last changes fastest.
Arguments:
- tokens: bfloat16 [4, 4096, 1024], P('shard', 'ctx'), may hold values from -6 to 6
- lengths: int32 [4], P('shard'), may hold values from 1024 to 4096, as said below
- routes: int32 [4, 4096, 1], P('shard', 'ctx'), may hold values from 0 to 15
- query_key_value_weight: bfloat16 [3, 1024, 1024], P(None, ('shard', 'ctx'), 'tp'), may hold values from -0.1875 to 0.1875
- context_blend_linear_map: bfloat16 [1024, 1024], P(('shard', 'ctx'), 'tp'), may hold values from -3 to 3
- router: bfloat16 [1024, 16], P(('shard', 'ctx')), may hold values from -0.09375 to 0.09375
- gain_one: bfloat16 [1024], P(('shard', 'ctx')), may hold values from 0.5 to 1.5
- gain_two: bfloat16 [1024], P(('shard', 'ctx')), may hold values from 0.5 to 1.5
- w_in: bfloat16 [16, 1024, 4096], P(('shard', 'ctx'), None, 'tp'), may hold values from -0.1875 to 0.1875
- w_out: bfloat16 [16, 4096, 1024], P(('shard', 'ctx'), 'tp'), may hold values from -1.5 to 1.5
- cotangent: bfloat16 [4, 4096, 1024], P('shard', 'ctx'), may hold values from -6 to 6
Outputs:
- output: bfloat16 [4, 4096, 1024], P('shard', 'ctx')
- grad_tokens: float32 [4, 4096, 1024], P('shard', 'ctx')
- grad_w_qkv: float32 [3, 1024, 1024], P(None, ('shard', 'ctx'), 'tp')
- grad_attn_proj: float32 [1024, 1024], P(('shard', 'ctx'), 'tp')
- grad_router: float32 [1024, 16], P(('shard', 'ctx'))
- grad_gain_one: float32 [1024], P(('shard', 'ctx'))
- grad_gain_two: float32 [1024], P(('shard', 'ctx'))
- grad_w_in: float32 [16, 1024, 4096], P(('shard', 'ctx'), None, 'tp')
- grad_w_out: float32 [16, 4096, 1024], P(('shard', 'ctx'), 'tp')
The draws below stay inside these ranges and needn't reach their ends.
Inputs may be any that keep to these rules, and one draw needn't show every extreme that they name: `lengths`: at least one slot has all 4096 positions used.
All inputs are finite; a program needn't handle non-finite values.
Results may differ from the reference program's by a relative error of at most 0.03.
Values may be sent and summed in bfloat16 or wider, within the bound.
A program may use at most 256 MiB of HBM per device.

```python
import jax
import jax.numpy as jnp
from jax import lax

D = 1024
HEADS = 16
HEAD_DIM = 64
FF = 4096
LC = 1024
SLOTS_DEV = 1
EXPERTS = 16
DEVICE_TEAMS = 16
LEN = 4096
SLOTS = 4
TOK_DEV = 1024
CAP = 80
N_SHARD = 4
N_CTX = 4


def draw_lengths(key, part):
    first_key, second_key = jax.random.split(jax.random.fold_in(key, 17))
    drawn = jax.random.randint(first_key, (SLOTS,), LEN // 4, LEN + 1)
    chosen = jax.random.randint(second_key, (), 0, SLOTS)
    return jnp.where(jnp.arange(SLOTS) == chosen, LEN, drawn).astype(jnp.int32)


def strengthened(values, key, source, target, parts, factor):
    def block_of(axis_at):
        return (jnp.arange(values.shape[axis_at]) // (values.shape[axis_at] // parts)).reshape((-1,) + (1,) * (values.ndim - 1 - axis_at))

    near = jax.random.permutation(key, parts)[block_of(target)]
    far = (block_of(target) + parts // 2) % parts
    return jnp.where((block_of(source) == near) | (block_of(source) == far), factor * values, values)


def shard_levels(stream_key, extent, cuts, low, largest):
    def one(axis_at, blocks):
        draws = jax.random.uniform(jax.random.fold_in(jax.random.fold_in(stream_key, 6), axis_at), (blocks,), jnp.float32, low / len(cuts), largest / len(cuts))
        return jnp.repeat(jnp.exp(draws), extent[axis_at] // blocks).reshape((-1,) + (1,) * (len(extent) - axis_at - 1))

    loudness = one(*cuts[0])
    for cut in cuts[1:]:
        loudness = loudness * one(*cut)
    return loudness


def choose_distinct(stream_key, rows, count, top, lift):
    order = jax.random.permutation(jax.random.fold_in(stream_key, 1), count)
    favour = order
    for power in range(3):
        favour = favour * favour // count
    favour = favour * lift // count
    lots = jax.random.randint(jax.random.fold_in(stream_key, 2), (rows, count), 0, 4096) + favour
    fixed_rows = jax.random.permutation(jax.random.fold_in(stream_key, 3), rows)[jnp.arange(count) % rows]
    lots = jnp.where(jnp.arange(rows)[:, None] == fixed_rows[None, :], 1 << 14, lots)
    score = lots * count + jnp.arange(count)
    return lax.top_k(score.astype(jnp.int32), top)[1].astype(jnp.int32)


def gaussian(own_key, extent, scale, limit, cuts=(), kind=jnp.bfloat16):
    values = scale * jax.random.normal(own_key, extent, jnp.float32)
    if cuts:
        values = values * shard_levels(own_key, extent, cuts, -0.22, 0.18)
    return jnp.clip(values, -limit, limit).astype(kind)


def gaussian_with(own_key, extent, scale, most, shards, heavy, kind=jnp.bfloat16):
    values = scale * jax.random.normal(own_key, extent, jnp.float32)
    if shards:
        values = values * shard_levels(own_key, extent, shards, -0.22, 0.18)
    return jnp.clip(strengthened(values, jax.random.fold_in(own_key, 3), *heavy), -most, most).astype(kind)


def setup_inputs(seed: int = 0) -> dict:
    key_of = jax.random.split(jax.random.key(seed), 12)
    return {
        "tokens": gaussian(key_of[0], (SLOTS, LEN, D), 1.0, 6.0, ((0, 4), (1, 4))),
        "lengths": draw_lengths(jax.random.fold_in(key_of[11], 71), 0),
        "routes": choose_distinct(key_of[2], SLOTS * LEN, EXPERTS, 1, 512).reshape((SLOTS, LEN, 1)),
        "query_key_value_weight": gaussian(key_of[3], (3, D, HEADS * HEAD_DIM), D ** -0.5, 0.1875, ((1, 16), (2, 2))),
        "context_blend_linear_map": gaussian(key_of[4], (D, HEADS * HEAD_DIM), (max(HEADS * HEAD_DIM // 256, 1)) ** -0.5, 3.0, ((0, 16), (1, 2))),
        "router": gaussian(key_of[5], (D, EXPERTS), (4 * D) ** -0.5, 0.09375, ((0, 16),)),
        "gain_one": jnp.clip(1.0 + 0.1 * jax.random.normal(key_of[6], (D,), jnp.float32), 0.5, 1.5).astype(jnp.bfloat16),
        "gain_two": jnp.clip(1.0 + 0.1 * jax.random.normal(key_of[7], (D,), jnp.float32), 0.5, 1.5).astype(jnp.bfloat16),
        "w_in": gaussian(key_of[8], (EXPERTS, D, FF), D ** -0.5, 0.1875, ((0, 16), (2, 2))),
        "w_out": gaussian(key_of[9], (EXPERTS, FF, D), (max(FF // (EXPERTS * EXPERTS), 1)) ** -0.5, 1.5, ((0, 16), (1, 2))),
        "cotangent": gaussian_with(key_of[10], (SLOTS, LEN, D), 1.0, 6.0, ((0, 4), (1, 4)), (0, 2, 4, 2.0)),
    }


@jax.custom_vjp
def low(v):
    return lax.optimization_barrier(v.astype(jnp.bfloat16)).astype(jnp.float32)

@jax.custom_vjp
def summed_cotangent_pass(v):
    return v

def low_keep(v):
    return (low(v), None)

def low_pass(kept, grad):
    return (grad,)

def back_keep(v):
    return (v, None)

def back_low(kept, grad):
    return (low(grad),)
low.defvjp(low_keep, low_pass)
summed_cotangent_pass.defvjp(back_keep, back_low)
epsilon = 1e-05
exact_arithmetic_mode = lax.Precision.HIGHEST
masked_score = -1e+30

def layer_norm(values, gain):
    center = values - lax.optimization_barrier(jnp.mean(values, axis=-1, keepdims=True))
    spread = lax.optimization_barrier(jnp.mean(center * center, axis=-1, keepdims=True))
    return center * lax.rsqrt(spread + epsilon) * gain

def to_groups(array):
    rest = array.shape[2:]
    shaped = array.reshape((N_SHARD, SLOTS_DEV, N_CTX, LC) + rest)
    return jnp.swapaxes(shaped, 1, 2).reshape((DEVICE_TEAMS * TOK_DEV,) + rest)

def from_groups(array):
    rest = array.shape[1:]
    shaped = array.reshape((N_SHARD, N_CTX, SLOTS_DEV, LC) + rest)
    return jnp.swapaxes(shaped, 1, 2).reshape((SLOTS, LEN) + rest)

def routing(lengths, routes):
    places = jnp.arange(LEN, dtype=jnp.int32)
    valid = (places[None, :] < lengths[:, None]).astype(jnp.int32)
    route_grp = to_groups(routes[:, :, 0]).reshape(DEVICE_TEAMS, TOK_DEV)
    valid_grp = to_groups(valid).reshape(DEVICE_TEAMS, TOK_DEV)
    expert_ids = jnp.arange(EXPERTS, dtype=jnp.int32)
    onehot = (route_grp[:, :, None] == expert_ids[None, None, :]).astype(jnp.int32) * valid_grp[:, :, None]
    earlier = jnp.cumsum(onehot, axis=1) - onehot
    place = lax.optimization_barrier(jnp.sum(earlier * onehot, axis=2))
    kept = valid_grp * (place < CAP).astype(jnp.int32)
    source = jnp.arange(DEVICE_TEAMS, dtype=jnp.int32)[:, None]
    target = jnp.where(kept > 0, route_grp * (DEVICE_TEAMS * CAP) + source * CAP + place, EXPERTS * DEVICE_TEAMS * CAP)
    return (valid, kept.reshape(DEVICE_TEAMS * TOK_DEV), target.reshape(DEVICE_TEAMS * TOK_DEV).astype(jnp.int32))

def layer(tokens, query_key_value_weight, context_blend_linear_map, router, gain_one, gain_two, w_in, w_out, lengths, routes, valid, kept, target):
    first_part = low(layer_norm(tokens, gain_one))
    projected_rows = jnp.einsum('oyu,vuj->oyvj', first_part, query_key_value_weight, precision=exact_arithmetic_mode)
    projected_rows = summed_cotangent_pass(low(projected_rows))
    shaped = projected_rows.reshape(SLOTS, LEN, 3, HEADS, HEAD_DIM)
    scale = HEAD_DIM ** (-0.5)
    places = jnp.arange(LEN, dtype=jnp.int32)
    causal = places[None, :] <= places[:, None]

    def attend(pieces):
        queries, keys, values, length = pieces
        allowed = causal & (places[None, :] < length)
        scores = summed_cotangent_pass(jnp.einsum('qhd,khd->hqk', queries, keys, precision=exact_arithmetic_mode) * scale)
        scores = jnp.where(allowed[None], scores, masked_score)
        weights = low(jax.nn.softmax(scores, axis=-1))
        return jnp.einsum('hqk,khd->qhd', weights, values, precision=exact_arithmetic_mode)
    attended = lax.map(jax.checkpoint(attend), (shaped[:, :, 0], shaped[:, :, 1], shaped[:, :, 2], lengths))
    blended_layer_yield = summed_cotangent_pass(low(attended.reshape(SLOTS, LEN, HEADS * HEAD_DIM)))
    expert_path_yield = summed_cotangent_pass(jnp.einsum('tuf,qf->tuq', blended_layer_yield, context_blend_linear_map, precision=exact_arithmetic_mode))
    middle = tokens + expert_path_yield
    second_part = low(layer_norm(middle, gain_two))
    router_logits = summed_cotangent_pass(jnp.einsum('vpq,qw->vpw', second_part, router, precision=exact_arithmetic_mode))
    probs = jax.nn.softmax(router_logits, axis=-1)
    gate = jnp.take_along_axis(probs, routes, axis=-1)[..., 0]
    rows = to_groups(second_part)
    buffer = jnp.zeros((EXPERTS * DEVICE_TEAMS * CAP + 1, D), jnp.float32).at[target].add(rows)
    dispatched = summed_cotangent_pass(buffer[:-1].reshape(EXPERTS, DEVICE_TEAMS * CAP, D))

    def expert(pieces):
        inputs, first_w, second_w = pieces
        pre = summed_cotangent_pass(jnp.dot(inputs, first_w, precision=exact_arithmetic_mode))
        hidden = low(jax.nn.gelu(pre))
        return summed_cotangent_pass(low(jnp.dot(hidden, second_w, precision=exact_arithmetic_mode)))
    returned = lax.map(jax.checkpoint(expert), (dispatched, w_in, w_out))
    padded = jnp.concatenate([returned.reshape(EXPERTS * DEVICE_TEAMS * CAP, D), jnp.zeros((1, D), jnp.float32)], axis=0)
    fetched = from_groups(padded[target])
    kept_slots = from_groups(kept).astype(jnp.float32)
    moe = (kept_slots * gate)[..., None] * fetched
    return valid.astype(jnp.float32)[..., None] * (middle + moe)

def reference(tokens, lengths, routes, query_key_value_weight, context_blend_linear_map, router, gain_one, gain_two, w_in, w_out, cotangent):
    valid, kept, target = routing(lengths, routes)

    def finished_flag(tokens_f, qkv_f, proj_f, router_f, one_f, two_f, in_f, out_f):
        return layer(tokens_f, qkv_f, proj_f, router_f, one_f, two_f, in_f, out_f, lengths, routes, valid, kept, target)
    primals = tuple((array.astype(jnp.float32) for array in (tokens, query_key_value_weight, context_blend_linear_map, router, gain_one, gain_two, w_in, w_out)))
    output, backward = jax.vjp(finished_flag, *primals)
    grads = backward(cotangent.astype(jnp.float32))
    return (output.astype(jnp.bfloat16), grads[0], grads[1], grads[2], grads[3], grads[4], grads[5], grads[6], grads[7])
```

```python
import functools

import jax
import jax.numpy as jnp
from jax import lax
from jax.experimental import pallas as pl
from jax.experimental.pallas import tpu as pltpu
from jax.sharding import PartitionSpec as P

HEAD_DIM = 64
EPSILON = 1e-05
MASKED = -1e30
LOG2E = 1.4426950408889634
BLOCK = 512
MESH = pl.DeviceIdType.MESH
BF16 = jnp.bfloat16
F32 = jnp.float32


class Item:
    def __init__(self, group, ins, outs, src, dst, relay=None, block=None, keep=True):
        self.group, self.ins, self.outs = group, ins, outs
        self.src, self.dst, self.relay, self.block, self.keep = src, dst, relay, block, keep


def exchange(name, collective_id, sizes, items):
    shards, ctxs, tps = sizes
    count_all = shards * ctxs
    operands = [item.ins for item in items]
    out_shapes = [shape for item in items for shape in item.outs]
    scratch = []
    for item in items:
        n = {"ctx": ctxs, "all": count_all, "pair": 1}[item.group]
        item.n = n
        scratch += [pltpu.SemaphoreType.DMA((n,)) for _ in range(4)]
        scratch.append(pltpu.SemaphoreType.DMA((2,)))
        if item.keep:
            scratch.append(pltpu.VMEM(item.block, item.ins.dtype))
    wide = any(item.group == "all" for item in items)
    near = any(item.group == "ctx" for item in items)
    paired = any(item.group == "pair" or item.relay is not None for item in items)

    def body(*refs):
        in_refs = refs[: len(operands)]
        out_refs = refs[len(operands) : len(operands) + len(out_shapes)]
        rest = list(refs[len(operands) + len(out_shapes) :])
        me_s, me_c, me_t = lax.axis_index("shard"), lax.axis_index("ctx"), lax.axis_index("tp")
        me_all = me_s * ctxs + me_c
        other = tps - 1 - me_t
        partner = {"tp": other}

        def place(group, p):
            if group == "ctx":
                return {"ctx": p}
            return {"shard": p // ctxs, "ctx": p % ctxs}

        barrier = pltpu.get_barrier_semaphore()
        group, size, me = ("all", count_all, me_all) if wide else ("ctx", ctxs, me_c)
        greeted = 0
        if wide or near:

            def greet(k, carry):
                peer = lax.rem(me + k, size)
                pl.semaphore_signal(
                    barrier, inc=1, device_id=place(group, peer), device_id_type=MESH
                )
                return carry

            lax.fori_loop(1, size, greet, 0)
            greeted += size - 1
        if paired:
            pl.semaphore_signal(barrier, inc=1, device_id=partner, device_id_type=MESH)
            greeted += 1
        pl.semaphore_wait(barrier, greeted)

        jobs = []
        at = 0
        for item, source in zip(items, in_refs):
            outs = out_refs[at : at + len(item.outs)]
            at += len(item.outs)
            sems = [rest.pop(0) for _ in range(5)]
            stage = rest.pop(0) if item.keep else None
            jobs.append((item, source, outs, sems, stage))

        def make(item, source, outs, sems, k, peer, sender):
            mine = {"ctx": me_c, "all": me_all}[item.group]
            return pltpu.make_async_remote_copy(
                src_ref=item.src(source, peer),
                dst_ref=item.dst(outs[0], sender, me_t),
                send_sem=sems[0].at[k],
                recv_sem=sems[1].at[sender],
                device_id=place(item.group, peer),
                device_id_type=MESH,
            )

        def make_relay(item, source, outs, sems, k, member, first):
            mine = {"ctx": me_c, "all": me_all, "pair": 0}[item.group]
            return pltpu.make_async_remote_copy(
                src_ref=item.src(source, mine) if first else item.dst(outs[0], member, me_t),
                dst_ref=item.relay(outs[-1], member, me_t),
                send_sem=sems[2].at[k],
                recv_sem=sems[3].at[member],
                device_id=partner,
                device_id_type=MESH,
            )

        def each(n, act):
            def step(k, carry):
                act(k)
                return carry

            lax.fori_loop(1, n, step, 0)

        mine_of = {"ctx": me_c, "all": me_all, "pair": 0}
        for item, source, outs, sems, stage in jobs:
            mine = mine_of[item.group]
            if item.n > 1:

                def send(k, item=item, source=source, outs=outs, sems=sems, mine=mine):
                    peer = lax.rem(mine + k, item.n)
                    make(item, source, outs, sems, k, peer, mine).start()

                each(item.n, send)
            if item.relay is not None:
                make_relay(item, source, outs, sems, 0, mine, True).start()
        for item, source, outs, sems, stage in jobs:
            if item.keep:
                pltpu.make_async_copy(
                    item.src(source, mine_of[item.group]), stage, sems[4].at[0]
                ).start()
        for item, source, outs, sems, stage in jobs:
            if item.keep:
                mine = mine_of[item.group]
                pltpu.make_async_copy(item.src(source, mine), stage, sems[4].at[0]).wait()
                pltpu.make_async_copy(
                    stage, item.dst(outs[0], mine, me_t), sems[4].at[1]
                ).start()
        for item, source, outs, sems, stage in jobs:
            mine = mine_of[item.group]
            if item.n > 1:

                def take(k, item=item, source=source, outs=outs, sems=sems, mine=mine):
                    member = lax.rem(mine + item.n - k, item.n)
                    peer = lax.rem(mine + k, item.n)
                    make(item, source, outs, sems, k, peer, member).wait_recv()
                    if item.relay is not None:
                        make_relay(item, source, outs, sems, k, member, False).start()

                each(item.n, take)
        for item, source, outs, sems, stage in jobs:
            mine = mine_of[item.group]
            if item.n > 1:

                def sent(k, item=item, source=source, outs=outs, sems=sems, mine=mine):
                    peer = lax.rem(mine + k, item.n)
                    make(item, source, outs, sems, k, peer, mine).wait_send()

                each(item.n, sent)
            if item.relay is not None:
                make_relay(item, source, outs, sems, 0, mine, True).wait()
                if item.n > 1:

                    def passed(k, item=item, source=source, outs=outs, sems=sems, mine=mine):
                        member = lax.rem(mine + item.n - k, item.n)
                        make_relay(item, source, outs, sems, k, member, False).wait()

                    each(item.n, passed)
            if item.keep:
                pltpu.make_async_copy(
                    stage, item.dst(outs[0], mine, me_t), sems[4].at[1]
                ).wait()

    anywhere = pl.BlockSpec(memory_space=pl.ANY)
    return pl.pallas_call(
        body,
        name=name,
        out_shape=tuple(out_shapes),
        in_specs=[anywhere] * len(operands),
        out_specs=tuple([anywhere] * len(out_shapes)),
        scratch_shapes=scratch,
        compiler_params=pltpu.CompilerParams(collective_id=collective_id, has_side_effects=True),
    )(*operands)


def nt(left, right):
    return lax.dot_general(left, right, (((1,), (1,)), ((), ())), preferred_element_type=F32)


def nn(left, right):
    return lax.dot_general(left, right, (((1,), (0,)), ((), ())), preferred_element_type=F32)


def tn(left, right):
    return lax.dot_general(left, right, (((0,), (0,)), ((), ())), preferred_element_type=F32)


def stacked(rows, heads):
    lane = lax.broadcasted_iota(jnp.int32, rows.shape, 1) // HEAD_DIM
    return jnp.concatenate([jnp.where(lane == h, rows, jnp.zeros_like(rows)) for h in range(heads)], 0)


def merged(pieces, heads):
    block = pieces.shape[0] // heads
    lane = lax.broadcasted_iota(jnp.int32, (block, pieces.shape[1]), 1) // HEAD_DIM
    total = pieces[:block]
    for h in range(1, heads):
        total = jnp.where(lane == h, pieces[h * block : (h + 1) * block], total)
    return total


def forward_kernel(heads, size, len_ref, q_ref, k_ref, v_ref, o_ref, lse_ref):
    i = pl.program_id(0)
    length = len_ref[0]
    scale = HEAD_DIM ** (-0.5)
    queries = stacked((q_ref[...].astype(F32) * scale).astype(BF16), heads)
    tall = heads * size
    row = lax.broadcasted_iota(jnp.int32, (tall, 1), 0) % size
    limit = jnp.minimum(i * size + row, length - 1)
    full = (jnp.minimum(i * size, length - 1) + 1) // size
    every = (jnp.minimum((i + 1) * size, length) + size - 1) // size

    def step(masked, j, state):
        top, total, accum = state
        place = pl.ds(pl.multiple_of(j * size, size), size)
        scores = nt(queries, k_ref[place, :]) * LOG2E
        if masked:
            column = j * size + lax.broadcasted_iota(jnp.int32, (tall, size), 1)
            scores = jnp.where(column <= limit, scores, MASKED)
        new_top = jnp.maximum(top, jnp.max(scores, axis=-1, keepdims=True))
        factor = jnp.exp2(top - new_top)
        weights = jnp.exp2(scores - new_top)
        total = total * factor + jnp.sum(weights, axis=-1, keepdims=True)
        accum = accum * factor + nn(weights.astype(BF16), v_ref[place, :])
        return new_top, total, accum

    state = (
        jnp.full((tall, 1), MASKED, F32),
        jnp.zeros((tall, 1), F32),
        jnp.zeros((tall, heads * HEAD_DIM), F32),
    )
    state = lax.fori_loop(0, full, functools.partial(step, False), state)
    top, total, accum = lax.fori_loop(full, every, functools.partial(step, True), state)
    o_ref[...] = merged(accum / total, heads).astype(BF16)
    log_total = jnp.broadcast_to(top + jnp.log2(total), (tall, 128))
    lse_ref[0] = jnp.transpose(log_total)[:1, :]


def attention_forward(projected, lengths, heads):
    count, _ = projected.shape
    wide = heads * HEAD_DIM
    size = BLOCK
    blocks = count // size
    return pl.pallas_call(
        functools.partial(forward_kernel, heads, size),
        name="attention_forward",
        out_shape=(
            jax.ShapeDtypeStruct((count, wide), BF16),
            jax.ShapeDtypeStruct((blocks, 1, heads * size), F32),
        ),
        grid_spec=pltpu.PrefetchScalarGridSpec(
            num_scalar_prefetch=1,
            grid=(blocks,),
            in_specs=[
                pl.BlockSpec((size, wide), lambda i, n: (i, 0)),
                pl.BlockSpec((count, wide), lambda i, n: (0, 1)),
                pl.BlockSpec((count, wide), lambda i, n: (0, 2)),
            ],
            out_specs=[
                pl.BlockSpec((size, wide), lambda i, n: (i, 0)),
                pl.BlockSpec((1, 1, heads * size), lambda i, n: (i, 0, 0)),
            ],
        ),
        cost_estimate=pl.CostEstimate(
            flops=16 * count * count * wide,
            bytes_accessed=8 * count * wide,
            transcendentals=heads * count * count // 2,
        ),
    )(lengths, projected, projected, projected)


def backward_kernel(
    heads, size, blocks, len_ref, q_ref, k_ref, v_ref, o_ref, do_ref, lse_ref, out_ref,
    queries, grads, delta, grad_queries,
):
    j = pl.program_id(0)
    length = len_ref[0]
    scale = HEAD_DIM ** (-0.5)
    tall = heads * size
    wide = heads * HEAD_DIM

    @pl.when(j == 0)
    def _():
        def prepare(i, carry):
            place = pl.ds(pl.multiple_of(i * size, size), size)
            tall_place = pl.ds(pl.multiple_of(i * tall, tall), tall)
            queries[tall_place, :] = stacked((q_ref[place, :].astype(F32) * scale).astype(BF16), heads)
            grad = do_ref[place, :]
            grads[tall_place, :] = stacked(grad, heads)
            product = jnp.transpose(grad.astype(F32) * o_ref[place, :].astype(F32))
            delta[i] = jnp.concatenate(
                [
                    jnp.sum(product[h * HEAD_DIM : (h + 1) * HEAD_DIM], axis=0, keepdims=True)
                    for h in range(heads)
                ],
                axis=1,
            )
            grad_queries[i] = jnp.zeros((wide, tall), F32)
            return carry

        lax.fori_loop(0, blocks, prepare, 0)

    keys = k_ref[...]
    values = v_ref[...]
    keys_turned = jnp.transpose(keys.astype(F32)).astype(BF16)
    column = j * size + lax.broadcasted_iota(jnp.int32, (size, tall), 0)
    inner = lax.broadcasted_iota(jnp.int32, (1, tall), 1) % size

    def step(masked, i, state):
        grad_keys, grad_values = state
        tall_place = pl.ds(pl.multiple_of(i * tall, tall), tall)
        query = queries[tall_place, :]
        grad = grads[tall_place, :]
        power = nt(keys, query) * LOG2E - lse_ref[i]
        if masked:
            limit = jnp.minimum(i * size + inner, length - 1)
            power = jnp.where(column <= limit, power, MASKED)
        weights = jnp.exp2(power)
        grad_values = grad_values + nn(weights.astype(BF16), grad)
        grad_scores = (weights * (nt(values, grad) - delta[i])).astype(BF16)
        grad_keys = grad_keys + nn(grad_scores, query)
        grad_queries[i] += nn(keys_turned, grad_scores)
        return grad_keys, grad_values

    state = (jnp.zeros((size, wide), F32), jnp.zeros((size, wide), F32))
    crosses = (j + 1) * size > length
    begin = jnp.where(j * size < length, j, blocks)
    middle = jnp.where(crosses, blocks, j + 1)
    state = lax.fori_loop(begin, middle, functools.partial(step, True), state)
    grad_keys, grad_values = lax.fori_loop(middle, blocks, functools.partial(step, False), state)
    place = pl.ds(pl.multiple_of(j * size, size), size)
    out_ref[place, wide : 2 * wide] = grad_keys.astype(BF16)
    out_ref[place, 2 * wide : 3 * wide] = grad_values.astype(BF16)

    @pl.when(j == blocks - 1)
    def _():
        def finish(i, carry):
            block_place = pl.ds(pl.multiple_of(i * size, size), size)
            turned = jnp.transpose(grad_queries[i])
            out_ref[block_place, :wide] = (merged(turned, heads) * scale).astype(BF16)
            return carry

        lax.fori_loop(0, blocks, finish, 0)


def attention_backward(projected, mixed, grad_mixed, lse, lengths, heads):
    count, _ = projected.shape
    wide = heads * HEAD_DIM
    size = BLOCK
    blocks = count // size
    tall = heads * size
    return pl.pallas_call(
        functools.partial(backward_kernel, heads, size, blocks),
        name="attention_backward",
        out_shape=jax.ShapeDtypeStruct((count, 3 * wide), BF16),
        grid_spec=pltpu.PrefetchScalarGridSpec(
            num_scalar_prefetch=1,
            grid=(blocks,),
            in_specs=[
                pl.BlockSpec((count, wide), lambda j, n: (0, 0)),
                pl.BlockSpec((size, wide), lambda j, n: (j, 1)),
                pl.BlockSpec((size, wide), lambda j, n: (j, 2)),
                pl.BlockSpec((count, wide), lambda j, n: (0, 0)),
                pl.BlockSpec((count, wide), lambda j, n: (0, 0)),
                pl.BlockSpec((blocks, 1, tall), lambda j, n: (0, 0, 0)),
            ],
            out_specs=pl.BlockSpec((count, 3 * wide), lambda j, n: (0, 0)),
            scratch_shapes=[
                pltpu.VMEM((heads * count, wide), BF16),
                pltpu.VMEM((heads * count, wide), BF16),
                pltpu.VMEM((blocks, 1, tall), F32),
                pltpu.VMEM((blocks, wide, tall), F32),
            ],
        ),
        cost_estimate=pl.CostEstimate(
            flops=40 * count * count * wide,
            bytes_accessed=16 * count * wide,
            transcendentals=heads * count * count // 2,
        ),
    )(lengths, projected, projected, projected, mixed, grad_mixed, lse)


def normed(values):
    center = values - jnp.mean(values, axis=-1, keepdims=True)
    inverse = lax.rsqrt(jnp.mean(center * center, axis=-1, keepdims=True) + EPSILON)
    return center * inverse, inverse


def norm_back(scaled, unit, inverse):
    return inverse * (
        scaled
        - jnp.mean(scaled, axis=-1, keepdims=True)
        - unit * jnp.mean(scaled * unit, axis=-1, keepdims=True)
    )


def shape_of(extent, dtype):
    return jax.ShapeDtypeStruct(extent, dtype)


def local(
    sizes, tokens, lengths, routes, weight_qkv, weight_proj, router, gain_one, gain_two,
    w_in, w_out, cotangent,
):
    shards, ctxs, tps = sizes
    group = ("shard", "ctx")
    groups = shards * ctxs
    slots, count, width = tokens.shape
    assert slots == 1 and tps == 2
    head_width = weight_qkv.shape[2]
    wide = head_width // ctxs
    heads = wide // HEAD_DIM
    rows = weight_qkv.shape[1]
    experts = router.shape[1]
    capacity = max(2, (5 * count + 4 * experts - 1) // (4 * experts))
    assert capacity % 2 == 0
    half_cap = capacity // 2
    half = count // tps
    length_all = ctxs * count
    ctx_rank = lax.axis_index("ctx")
    tp_rank = lax.axis_index("tp")

    inputs = tokens[0].astype(F32)
    own_half = lax.dynamic_slice_in_dim(tokens[0], tp_rank * half, half, 0).astype(F32)
    unit_half = normed(own_half)[0].astype(BF16)
    scaled_qkv = (weight_qkv.astype(F32) * gain_one.astype(F32)[None, :, None]).astype(BF16)
    by_ctx = scaled_qkv.reshape(3, rows, ctxs, wide).transpose(2, 1, 0, 3).reshape(ctxs, rows, 3 * wide)
    pad = -(-(experts + 1) // 128) * 128
    small = jnp.concatenate(
        [router, gain_two[:, None], jnp.zeros((rows, pad - experts - 1), BF16)], axis=1
    )
    sent_weights = jnp.concatenate(
        [by_ctx, jnp.broadcast_to(small[None], (ctxs, rows, pad))], axis=2
    )
    whole_qkv = lax.all_gather(
        by_ctx.transpose(1, 0, 2).reshape(rows, ctxs * 3 * wide), group, axis=0, tiled=True
    )
    whole_proj = lax.all_gather(weight_proj, group, axis=0, tiled=True)

    unit_all, got_weights = exchange(
        "gather_rows", 1, sizes,
        [
            Item(
                "ctx", unit_half, [shape_of((ctxs, tps, half, width), BF16)],
                lambda ref, p: ref,
                lambda ref, q, t: ref.at[q, t],
                relay=lambda ref, q, t: ref.at[q, t],
                block=(half, width),
            ),
            Item(
                "all", sent_weights, [shape_of((groups, rows, 3 * wide + pad), BF16)],
                lambda ref, p: ref.at[p % ctxs],
                lambda ref, q, t: ref.at[q],
                block=(rows, 3 * wide + pad),
            ),
        ],
    )
    unit_all = unit_all.reshape(length_all, width)
    got_weights = got_weights.reshape(width, 3 * wide + pad)
    own_qkv = got_weights[:, : 3 * wide]
    full_router = got_weights[:, 3 * wide : 3 * wide + experts]
    full_two = got_weights[:, 3 * wide + experts].astype(F32)

    places = ctx_rank * count + jnp.arange(count, dtype=jnp.int32)
    route = routes.reshape(count)
    valid = places < lengths[0]
    route_hot = route[:, None] == jnp.arange(experts, dtype=jnp.int32)[None, :]
    counted = (route_hot & valid[:, None]).astype(BF16)
    order = jnp.arange(count, dtype=jnp.int32)
    below = (order[:, None] > order[None, :]).astype(BF16)
    earlier = nn(below, counted)
    place = jnp.sum(earlier * counted.astype(F32), axis=1).astype(jnp.int32)
    kept = valid & (place < capacity)
    target = jnp.where(kept, route * capacity + place, experts * capacity)
    slot = jnp.arange(experts * half_cap, dtype=jnp.int32)
    slot = (slot // half_cap) * capacity + slot % half_cap
    own_slot = slot + tp_rank * half_cap
    par_slot = slot + (1 - tp_rank) * half_cap
    pick_own = (own_slot[:, None] == target[None, :]).astype(BF16)
    pick_par = (par_slot[:, None] == target[None, :]).astype(BF16)

    cot = cotangent[0]
    sent_cot = nn(pick_own, cot).astype(BF16).reshape(experts, half_cap, width)
    got_cot = lax.all_to_all(sent_cot, group, split_axis=0, concat_axis=0, tiled=True)

    projected = nn(unit_all, own_qkv).astype(BF16)
    mixed_heads, lse = attention_forward(projected, lengths, heads)

    mixed_own, mixed_par, proj_par, qkv_par, cot_par = exchange(
        "mixed_home", 2, sizes,
        [
            Item(
                "ctx", mixed_heads,
                [shape_of((count, head_width), BF16), shape_of((count, head_width), BF16)],
                lambda ref, p: ref.at[pl.ds(pl.multiple_of(p * count, count), count), :],
                lambda ref, q, t: ref.at[:, pl.ds(pl.multiple_of(q * wide, wide), wide)],
                relay=lambda ref, q, t: ref.at[:, pl.ds(pl.multiple_of(q * wide, wide), wide)],
                block=(count, wide),
            ),
            Item(
                "pair", whole_proj, [shape_of(whole_proj.shape, BF16)],
                lambda ref, p: ref, None, relay=lambda ref, q, t: ref, keep=False,
            ),
            Item(
                "pair", whole_qkv, [shape_of(whole_qkv.shape, BF16)],
                lambda ref, p: ref, None, relay=lambda ref, q, t: ref, keep=False,
            ),
            Item(
                "pair", got_cot, [shape_of(got_cot.shape, BF16)],
                lambda ref, p: ref, None, relay=lambda ref, q, t: ref, keep=False,
            ),
        ],
    )

    middle = inputs + nt(mixed_own, whole_proj) + nt(mixed_par, proj_par)
    unit_two, inverse_two = normed(middle)
    second = (unit_two * full_two).astype(BF16)
    probs = jax.nn.softmax(nn(second, full_router), axis=-1)
    gate = jnp.sum(jnp.where(route_hot, probs, 0.0), axis=1)
    sent_rows = nn(pick_own, second).astype(BF16).reshape(experts, half_cap, width)
    gate_rows = jnp.sum(
        jnp.where(own_slot[:, None] == target[None, :], gate[None, :], 0.0), axis=1
    ).reshape(experts, half_cap)
    lanes = -(-half_cap // 128) * 128
    gate_rows = jnp.broadcast_to(
        jnp.pad(gate_rows, ((0, 0), (0, lanes - half_cap)))[:, None, :], (experts, 8, lanes)
    )

    got_rows, got_gates = exchange(
        "dispatch", 3, sizes,
        [
            Item(
                "all", sent_rows, [shape_of((tps, groups, half_cap, width), BF16)],
                lambda ref, p: ref.at[p],
                lambda ref, q, t: ref.at[0, q],
                relay=lambda ref, q, t: ref.at[1, q],
                block=(half_cap, width),
            ),
            Item(
                "all", gate_rows, [shape_of((tps, groups, 8, lanes), F32)],
                lambda ref, p: ref.at[p],
                lambda ref, q, t: ref.at[0, q],
                relay=lambda ref, q, t: ref.at[1, q],
                block=(8, lanes),
            ),
        ],
    )

    total_rows = tps * groups * half_cap
    arrived = got_rows.reshape(total_rows, width)
    gates = got_gates[:, :, 0, :half_cap].reshape(total_rows)
    cot_rows = jnp.concatenate([got_cot, cot_par], axis=0).reshape(total_rows, width)
    grad_rows = (gates[:, None] * cot_rows.astype(F32)).astype(BF16)
    pre = nn(arrived, w_in[0])
    hidden, gelu_back = jax.vjp(jax.nn.gelu, pre)
    hidden = hidden.astype(BF16)
    partial_out = nn(hidden, w_out[0]).astype(BF16).reshape(tps, groups, half_cap, width)

    def pair_item(array, index):
        return Item(
            "pair", array, [shape_of(array.shape[1:], BF16)],
            lambda ref, p: ref.at[index], None, relay=lambda ref, q, t: ref, keep=False,
        )

    (out_par,) = exchange("sum_out", 4, sizes, [pair_item(partial_out, 1)])
    summed = (partial_out[0].astype(F32) + out_par.astype(F32)).astype(BF16)
    going_back = lax.all_to_all(summed, group, split_axis=0, concat_axis=0, tiled=True)

    grad_w_out = tn(hidden, grad_rows)[None]
    grad_hidden = nt(grad_rows, w_out[0])
    grad_pre = gelu_back(grad_hidden)[0].astype(BF16)
    partial_grad = nt(grad_pre, w_in[0]).astype(BF16).reshape(tps, groups, half_cap, width)
    grad_w_in = tn(arrived, grad_pre)[None]

    (grad_par,) = exchange("sum_grad", 5, sizes, [pair_item(partial_grad, 1)])
    grad_summed = (partial_grad[0].astype(F32) + grad_par.astype(F32)).astype(BF16)
    grad_home, back_par = exchange(
        "grad_home", 6, sizes,
        [
            Item(
                "all", grad_summed, [shape_of((tps, groups, half_cap, width), BF16)],
                lambda ref, p: ref.at[p],
                lambda ref, q, t: ref.at[0, q],
                relay=lambda ref, q, t: ref.at[1, q],
                block=(half_cap, width),
            ),
            Item(
                "pair", going_back, [shape_of(going_back.shape, BF16)],
                lambda ref, p: ref, None, relay=lambda ref, q, t: ref, keep=False,
            ),
        ],
    )

    slots_half = experts * half_cap
    fetched = tn(pick_own, going_back.reshape(slots_half, width)) + tn(
        pick_par, back_par.reshape(slots_half, width)
    )
    grad_home = grad_home.reshape(tps, slots_half, width)
    grad_home_rows = tn(pick_own, grad_home[0]) + tn(pick_par, grad_home[1])
    kept_value = kept.astype(F32)
    valid_value = valid.astype(F32)
    output = (
        (valid_value[:, None] * (middle + (kept_value * gate)[:, None] * fetched))
        .astype(BF16)
        .reshape(slots, count, width)
    )
    grad_out = valid_value[:, None] * cot.astype(F32)
    grad_gate = kept_value * jnp.sum(grad_out * fetched, axis=1)
    grad_logits = ((grad_gate * gate)[:, None] * (route_hot.astype(F32) - probs)).astype(BF16)
    grad_second = grad_home_rows + nt(grad_logits, full_router)
    grad_middle = grad_out + norm_back(grad_second * full_two, unit_two, inverse_two)
    grad_branch = grad_middle.astype(BF16)
    grad_mixed_own = nn(grad_branch, whole_proj).astype(BF16)

    (grad_mixed,) = exchange(
        "grad_mixed", 7, sizes,
        [
            Item(
                "ctx", grad_mixed_own, [shape_of((length_all, wide), BF16)],
                lambda ref, p: ref.at[:, pl.ds(pl.multiple_of(p * wide, wide), wide)],
                lambda ref, q, t: ref.at[pl.ds(pl.multiple_of(q * count, count), count), :],
                block=(count, wide),
            ),
        ],
    )
    grad_router = tn(second, grad_logits)
    grad_gain_two = jnp.sum(grad_second * unit_two, axis=0)
    grad_proj = tn(grad_branch, mixed_own)
    packed = jnp.concatenate(
        [grad_proj, grad_router, grad_gain_two[:, None], jnp.zeros((width, pad - experts - 1), F32)],
        axis=1,
    )
    owned = lax.psum_scatter(packed, group, scatter_dimension=0, tiled=True)
    owned_proj = owned[:, :head_width]
    owned_router = owned[:, head_width : head_width + experts]
    owned_two = owned[:, head_width + experts]

    grad_projected = attention_backward(projected, mixed_heads, grad_mixed, lse, lengths, heads)
    grad_weight = tn(unit_all, grad_projected).astype(BF16).reshape(groups, rows, 3 * wide)
    grad_own, grad_par, got_grad = exchange(
        "grad_projected", 8, sizes,
        [
            Item(
                "ctx", grad_projected,
                [shape_of((count, 3 * head_width), BF16), shape_of((count, 3 * head_width), BF16)],
                lambda ref, p: ref.at[pl.ds(pl.multiple_of(p * count, count), count), :],
                lambda ref, q, t: ref.at[:, pl.ds(pl.multiple_of(q * 3 * wide, wide), 3 * wide)],
                relay=lambda ref, q, t: ref.at[:, pl.ds(pl.multiple_of(q * 3 * wide, wide), 3 * wide)],
                block=(count, 3 * wide),
            ),
            Item(
                "all", grad_weight, [shape_of((groups, rows, 3 * wide), BF16)],
                lambda ref, p: ref.at[p],
                lambda ref, q, t: ref.at[q],
                block=(rows, 3 * wide),
            ),
        ],
    )
    scaled_first = nt(grad_own, whole_qkv) + nt(grad_par, qkv_par)
    unit_one, inverse_one = normed(inputs)
    grad_tokens = (grad_middle + norm_back(scaled_first, unit_one, inverse_one)).reshape(
        slots, count, width
    )
    raw = (
        jnp.sum(got_grad.astype(F32).reshape(shards, ctxs, rows, 3, wide), axis=0)
        .transpose(2, 1, 0, 3)
        .reshape(3, rows, head_width)
    )
    owned_qkv = raw * gain_one.astype(F32)[None, :, None]
    owned_one = lax.psum(jnp.sum(raw * weight_qkv.astype(F32), axis=(0, 2)), "tp")
    return (
        output,
        grad_tokens,
        owned_qkv,
        owned_proj,
        owned_router,
        owned_one,
        owned_two,
        grad_w_in,
        grad_w_out,
    )


def solution(mesh):
    sizes = (mesh.shape["shard"], mesh.shape["ctx"], mesh.shape["tp"])
    return jax.shard_map(
        functools.partial(local, sizes),
        mesh=mesh,
        in_specs=(
            P("shard", "ctx", None),
            P("shard"),
            P("shard", "ctx", None),
            P(None, ("shard", "ctx"), "tp"),
            P(("shard", "ctx"), "tp"),
            P(("shard", "ctx"), None),
            P(("shard", "ctx")),
            P(("shard", "ctx")),
            P(("shard", "ctx"), None, "tp"),
            P(("shard", "ctx"), "tp", None),
            P("shard", "ctx", None),
        ),
        out_specs=(
            P("shard", "ctx", None),
            P("shard", "ctx", None),
            P(None, ("shard", "ctx"), "tp"),
            P(("shard", "ctx"), "tp"),
            P(("shard", "ctx"), None),
            P(("shard", "ctx")),
            P(("shard", "ctx")),
            P(("shard", "ctx"), None, "tp"),
            P(("shard", "ctx"), "tp", None),
        ),
        check_vma=False,
    )
```

```python
import functools

import jax
import jax.numpy as jnp
from jax import lax
from jax.experimental import pallas as pl
from jax.experimental.pallas import tpu as pltpu
from jax.sharding import PartitionSpec as P

HEAD_DIM = 64
EPSILON = 1e-05
MASKED = -1e30
LOG2E = 1.4426950408889634
BLOCK = 512
MESH = pl.DeviceIdType.MESH
BF16 = jnp.bfloat16
F32 = jnp.float32


class Item:
    def __init__(self, group, ins, outs, src, dst, relay=None, block=None, keep=True):
        self.group, self.ins, self.outs = group, ins, outs
        self.src, self.dst, self.relay, self.block, self.keep = src, dst, relay, block, keep


def exchange(name, collective_id, sizes, items):
    shards, ctxs, tps = sizes
    count_all = shards * ctxs
    operands = [item.ins for item in items]
    out_shapes = [shape for item in items for shape in item.outs]
    scratch = []
    for item in items:
        n = {"ctx": ctxs, "all": count_all, "pair": 1}[item.group]
        item.n = n
        scratch += [pltpu.SemaphoreType.DMA((n,)) for _ in range(4)]
        scratch.append(pltpu.SemaphoreType.DMA((2,)))
        if item.keep:
            scratch.append(pltpu.VMEM(item.block, item.ins.dtype))
    wide = any(item.group == "all" for item in items)
    near = any(item.group == "ctx" for item in items)
    paired = any(item.group == "pair" or item.relay is not None for item in items)

    def body(*refs):
        in_refs = refs[: len(operands)]
        out_refs = refs[len(operands) : len(operands) + len(out_shapes)]
        rest = list(refs[len(operands) + len(out_shapes) :])
        me_s, me_c, me_t = lax.axis_index("shard"), lax.axis_index("ctx"), lax.axis_index("tp")
        me_all = me_s * ctxs + me_c
        other = tps - 1 - me_t
        partner = {"tp": other}

        def place(group, p):
            if group == "ctx":
                return {"ctx": p}
            return {"shard": p // ctxs, "ctx": p % ctxs}

        barrier = pltpu.get_barrier_semaphore()
        group, size, me = ("all", count_all, me_all) if wide else ("ctx", ctxs, me_c)
        greeted = 0
        if wide or near:

            def greet(k, carry):
                peer = lax.rem(me + k, size)
                pl.semaphore_signal(
                    barrier, inc=1, device_id=place(group, peer), device_id_type=MESH
                )
                return carry

            lax.fori_loop(1, size, greet, 0)
            greeted += size - 1
        if paired:
            pl.semaphore_signal(barrier, inc=1, device_id=partner, device_id_type=MESH)
            greeted += 1
        pl.semaphore_wait(barrier, greeted)

        jobs = []
        at = 0
        for item, source in zip(items, in_refs):
            outs = out_refs[at : at + len(item.outs)]
            at += len(item.outs)
            sems = [rest.pop(0) for _ in range(5)]
            stage = rest.pop(0) if item.keep else None
            jobs.append((item, source, outs, sems, stage))

        def make(item, source, outs, sems, k, peer, sender):
            mine = {"ctx": me_c, "all": me_all}[item.group]
            return pltpu.make_async_remote_copy(
                src_ref=item.src(source, peer),
                dst_ref=item.dst(outs[0], sender, me_t),
                send_sem=sems[0].at[k],
                recv_sem=sems[1].at[sender],
                device_id=place(item.group, peer),
                device_id_type=MESH,
            )

        def make_relay(item, source, outs, sems, k, member, first):
            mine = {"ctx": me_c, "all": me_all, "pair": 0}[item.group]
            return pltpu.make_async_remote_copy(
                src_ref=item.src(source, mine) if first else item.dst(outs[0], member, me_t),
                dst_ref=item.relay(outs[-1], member, me_t),
                send_sem=sems[2].at[k],
                recv_sem=sems[3].at[member],
                device_id=partner,
                device_id_type=MESH,
            )

        def each(n, act):
            def step(k, carry):
                act(k)
                return carry

            lax.fori_loop(1, n, step, 0)

        mine_of = {"ctx": me_c, "all": me_all, "pair": 0}
        for item, source, outs, sems, stage in jobs:
            mine = mine_of[item.group]
            if item.n > 1:

                def send(k, item=item, source=source, outs=outs, sems=sems, mine=mine):
                    peer = lax.rem(mine + k, item.n)
                    make(item, source, outs, sems, k, peer, mine).start()

                each(item.n, send)
            if item.relay is not None:
                make_relay(item, source, outs, sems, 0, mine, True).start()
        for item, source, outs, sems, stage in jobs:
            if item.keep:
                pltpu.make_async_copy(
                    item.src(source, mine_of[item.group]), stage, sems[4].at[0]
                ).start()
        for item, source, outs, sems, stage in jobs:
            if item.keep:
                mine = mine_of[item.group]
                pltpu.make_async_copy(item.src(source, mine), stage, sems[4].at[0]).wait()
                pltpu.make_async_copy(
                    stage, item.dst(outs[0], mine, me_t), sems[4].at[1]
                ).start()
        for item, source, outs, sems, stage in jobs:
            mine = mine_of[item.group]
            if item.n > 1:

                def take(k, item=item, source=source, outs=outs, sems=sems, mine=mine):
                    member = lax.rem(mine + item.n - k, item.n)
                    peer = lax.rem(mine + k, item.n)
                    make(item, source, outs, sems, k, peer, member).wait_recv()
                    if item.relay is not None:
                        make_relay(item, source, outs, sems, k, member, False).start()

                each(item.n, take)
        for item, source, outs, sems, stage in jobs:
            mine = mine_of[item.group]
            if item.n > 1:

                def sent(k, item=item, source=source, outs=outs, sems=sems, mine=mine):
                    peer = lax.rem(mine + k, item.n)
                    make(item, source, outs, sems, k, peer, mine).wait_send()

                each(item.n, sent)
            if item.relay is not None:
                make_relay(item, source, outs, sems, 0, mine, True).wait()
                if item.n > 1:

                    def passed(k, item=item, source=source, outs=outs, sems=sems, mine=mine):
                        member = lax.rem(mine + item.n - k, item.n)
                        make_relay(item, source, outs, sems, k, member, False).wait()

                    each(item.n, passed)
            if item.keep:
                pltpu.make_async_copy(
                    stage, item.dst(outs[0], mine, me_t), sems[4].at[1]
                ).wait()

    anywhere = pl.BlockSpec(memory_space=pl.ANY)
    return pl.pallas_call(
        body,
        name=name,
        out_shape=tuple(out_shapes),
        in_specs=[anywhere] * len(operands),
        out_specs=tuple([anywhere] * len(out_shapes)),
        scratch_shapes=scratch,
        compiler_params=pltpu.CompilerParams(collective_id=collective_id, has_side_effects=True),
    )(*operands)


def nt(left, right):
    return lax.dot_general(left, right, (((1,), (1,)), ((), ())), preferred_element_type=F32)


def nn(left, right):
    return lax.dot_general(left, right, (((1,), (0,)), ((), ())), preferred_element_type=F32)


def tn(left, right):
    return lax.dot_general(left, right, (((0,), (0,)), ((), ())), preferred_element_type=F32)


def stacked(rows, heads):
    lane = lax.broadcasted_iota(jnp.int32, rows.shape, 1) // HEAD_DIM
    return jnp.concatenate([jnp.where(lane == h, rows, jnp.zeros_like(rows)) for h in range(heads)], 0)


def merged(pieces, heads):
    block = pieces.shape[0] // heads
    lane = lax.broadcasted_iota(jnp.int32, (block, pieces.shape[1]), 1) // HEAD_DIM
    total = pieces[:block]
    for h in range(1, heads):
        total = jnp.where(lane == h, pieces[h * block : (h + 1) * block], total)
    return total


def forward_kernel(heads, size, span, spans, len_ref, q_ref, k_ref, v_ref, o_ref, lse_ref, turned):
    i = pl.program_id(0)
    length = len_ref[0]
    scale = HEAD_DIM ** (-0.5)
    tall = heads * size
    wide = heads * HEAD_DIM

    @pl.when(i == 0)
    def _():
        def turn(j, carry):
            place = pl.ds(pl.multiple_of(j * span, span), span)
            turned[j] = jnp.transpose(v_ref[place, :].astype(F32)).astype(BF16)
            return carry

        lax.fori_loop(0, spans, turn, 0)

    queries = stacked((q_ref[...].astype(F32) * scale).astype(BF16), heads)
    inner = lax.broadcasted_iota(jnp.int32, (1, tall), 1) % size
    limit = jnp.minimum(i * size + inner, length - 1)
    full = (jnp.minimum(i * size, length - 1) + 1) // span
    every = (jnp.minimum((i + 1) * size, length) + span - 1) // span

    def step(masked, j, state):
        top, total, accum = state
        place = pl.ds(pl.multiple_of(j * span, span), span)
        scores = nt(k_ref[place, :], queries) * LOG2E
        if masked:
            column = j * span + lax.broadcasted_iota(jnp.int32, (span, tall), 0)
            scores = jnp.where(column <= limit, scores, MASKED)
        new_top = jnp.maximum(top, jnp.max(scores, axis=0, keepdims=True))
        factor = jnp.exp2(top - new_top)
        weights = jnp.exp2(scores - new_top)
        total = total * factor + jnp.sum(weights, axis=0, keepdims=True)
        accum = accum * factor + nn(turned[j], weights.astype(BF16))
        return new_top, total, accum

    state = (
        jnp.full((1, tall), MASKED, F32),
        jnp.zeros((1, tall), F32),
        jnp.zeros((wide, tall), F32),
    )
    state = lax.fori_loop(0, full, functools.partial(step, False), state)
    top, total, accum = lax.fori_loop(full, every, functools.partial(step, True), state)
    o_ref[...] = merged(jnp.transpose(accum / total), heads).astype(BF16)
    lse_ref[0] = top + jnp.log2(total)


def attention_forward(projected, lengths, heads):
    count, _ = projected.shape
    wide = heads * HEAD_DIM
    size = BLOCK
    span = 2 * BLOCK
    blocks = count // size
    return pl.pallas_call(
        functools.partial(forward_kernel, heads, size, span, count // span),
        name="attention_forward",
        out_shape=(
            jax.ShapeDtypeStruct((count, wide), BF16),
            jax.ShapeDtypeStruct((blocks, 1, heads * size), F32),
        ),
        grid_spec=pltpu.PrefetchScalarGridSpec(
            num_scalar_prefetch=1,
            grid=(blocks,),
            in_specs=[
                pl.BlockSpec((size, wide), lambda i, n: (i, 0)),
                pl.BlockSpec((count, wide), lambda i, n: (0, 1)),
                pl.BlockSpec((count, wide), lambda i, n: (0, 2)),
            ],
            out_specs=[
                pl.BlockSpec((size, wide), lambda i, n: (i, 0)),
                pl.BlockSpec((1, 1, heads * size), lambda i, n: (i, 0, 0)),
            ],
            scratch_shapes=[pltpu.VMEM((count // span, wide, span), BF16)],
        ),
        cost_estimate=pl.CostEstimate(
            flops=16 * count * count * wide,
            bytes_accessed=8 * count * wide,
            transcendentals=heads * count * count // 2,
        ),
    )(lengths, projected, projected, projected)


def backward_kernel(
    heads, size, blocks, len_ref, q_ref, k_ref, v_ref, o_ref, do_ref, lse_ref, out_ref,
    queries, grads, delta, grad_queries,
):
    j = pl.program_id(0)
    length = len_ref[0]
    scale = HEAD_DIM ** (-0.5)
    tall = heads * size
    wide = heads * HEAD_DIM

    @pl.when(j == 0)
    def _():
        def prepare(i, carry):
            place = pl.ds(pl.multiple_of(i * size, size), size)
            tall_place = pl.ds(pl.multiple_of(i * tall, tall), tall)
            queries[tall_place, :] = stacked((q_ref[place, :].astype(F32) * scale).astype(BF16), heads)
            grad = do_ref[place, :]
            grads[tall_place, :] = stacked(grad, heads)
            product = jnp.transpose(grad.astype(F32) * o_ref[place, :].astype(F32))
            delta[i] = jnp.concatenate(
                [
                    jnp.sum(product[h * HEAD_DIM : (h + 1) * HEAD_DIM], axis=0, keepdims=True)
                    for h in range(heads)
                ],
                axis=1,
            )
            grad_queries[i] = jnp.zeros((wide, tall), F32)
            return carry

        lax.fori_loop(0, blocks, prepare, 0)

    keys = k_ref[...]
    values = v_ref[...]
    keys_turned = jnp.transpose(keys.astype(F32)).astype(BF16)
    column = j * size + lax.broadcasted_iota(jnp.int32, (size, tall), 0)
    inner = lax.broadcasted_iota(jnp.int32, (1, tall), 1) % size

    def step(masked, i, state):
        grad_keys, grad_values = state
        tall_place = pl.ds(pl.multiple_of(i * tall, tall), tall)
        query = queries[tall_place, :]
        grad = grads[tall_place, :]
        power = nt(keys, query) * LOG2E - lse_ref[i]
        if masked:
            limit = jnp.minimum(i * size + inner, length - 1)
            power = jnp.where(column <= limit, power, MASKED)
        weights = jnp.exp2(power)
        grad_values = grad_values + nn(weights.astype(BF16), grad)
        grad_scores = (weights * (nt(values, grad) - delta[i])).astype(BF16)
        grad_keys = grad_keys + nn(grad_scores, query)
        grad_queries[i] += nn(keys_turned, grad_scores)
        return grad_keys, grad_values

    state = (jnp.zeros((size, wide), F32), jnp.zeros((size, wide), F32))
    crosses = (j + 1) * size > length
    begin = jnp.where(j * size < length, j, blocks)
    middle = jnp.where(crosses, blocks, j + 1)
    state = lax.fori_loop(begin, middle, functools.partial(step, True), state)
    grad_keys, grad_values = lax.fori_loop(middle, blocks, functools.partial(step, False), state)
    place = pl.ds(pl.multiple_of(j * size, size), size)
    out_ref[place, wide : 2 * wide] = grad_keys.astype(BF16)
    out_ref[place, 2 * wide : 3 * wide] = grad_values.astype(BF16)

    @pl.when(j == blocks - 1)
    def _():
        def finish(i, carry):
            block_place = pl.ds(pl.multiple_of(i * size, size), size)
            turned = jnp.transpose(grad_queries[i])
            out_ref[block_place, :wide] = (merged(turned, heads) * scale).astype(BF16)
            return carry

        lax.fori_loop(0, blocks, finish, 0)


def attention_backward(projected, mixed, grad_mixed, lse, lengths, heads):
    count, _ = projected.shape
    wide = heads * HEAD_DIM
    size = BLOCK
    blocks = count // size
    tall = heads * size
    return pl.pallas_call(
        functools.partial(backward_kernel, heads, size, blocks),
        name="attention_backward",
        out_shape=jax.ShapeDtypeStruct((count, 3 * wide), BF16),
        grid_spec=pltpu.PrefetchScalarGridSpec(
            num_scalar_prefetch=1,
            grid=(blocks,),
            in_specs=[
                pl.BlockSpec((count, wide), lambda j, n: (0, 0)),
                pl.BlockSpec((size, wide), lambda j, n: (j, 1)),
                pl.BlockSpec((size, wide), lambda j, n: (j, 2)),
                pl.BlockSpec((count, wide), lambda j, n: (0, 0)),
                pl.BlockSpec((count, wide), lambda j, n: (0, 0)),
                pl.BlockSpec((blocks, 1, tall), lambda j, n: (0, 0, 0)),
            ],
            out_specs=pl.BlockSpec((count, 3 * wide), lambda j, n: (0, 0)),
            scratch_shapes=[
                pltpu.VMEM((heads * count, wide), BF16),
                pltpu.VMEM((heads * count, wide), BF16),
                pltpu.VMEM((blocks, 1, tall), F32),
                pltpu.VMEM((blocks, wide, tall), F32),
            ],
        ),
        cost_estimate=pl.CostEstimate(
            flops=40 * count * count * wide,
            bytes_accessed=16 * count * wide,
            transcendentals=heads * count * count // 2,
        ),
    )(lengths, projected, projected, projected, mixed, grad_mixed, lse)


def pair_sum(name, collective_id, partial):
    shape = partial.shape[1:]

    def body(in_ref, out_ref, own, got, sems):
        other = {"tp": 1 - lax.axis_index("tp")}
        barrier = pltpu.get_barrier_semaphore()
        pl.semaphore_signal(barrier, inc=1, device_id=other, device_id_type=MESH)
        pl.semaphore_wait(barrier, 1)
        away = pltpu.make_async_remote_copy(
            src_ref=in_ref.at[1],
            dst_ref=got,
            send_sem=sems.at[0],
            recv_sem=sems.at[1],
            device_id=other,
            device_id_type=MESH,
        )
        away.start()
        here = pltpu.make_async_copy(in_ref.at[0], own, sems.at[2])
        here.start()
        here.wait()
        away.wait()

        def add(e, carry):
            out_ref[e] = (own[e].astype(F32) + got[e].astype(F32)).astype(BF16)
            return carry

        lax.fori_loop(0, shape[0], add, 0)

    return pl.pallas_call(
        body,
        name=name,
        out_shape=jax.ShapeDtypeStruct(shape, BF16),
        in_specs=[pl.BlockSpec(memory_space=pl.ANY)],
        out_specs=pl.BlockSpec(memory_space=pltpu.VMEM),
        scratch_shapes=[
            pltpu.VMEM(shape, BF16),
            pltpu.VMEM(shape, BF16),
            pltpu.SemaphoreType.DMA((3,)),
        ],
        compiler_params=pltpu.CompilerParams(collective_id=collective_id, has_side_effects=True),
    )(partial)


def normed(values):
    center = values - jnp.mean(values, axis=-1, keepdims=True)
    inverse = lax.rsqrt(jnp.mean(center * center, axis=-1, keepdims=True) + EPSILON)
    return center * inverse, inverse


def norm_back(scaled, unit, inverse):
    return inverse * (
        scaled
        - jnp.mean(scaled, axis=-1, keepdims=True)
        - unit * jnp.mean(scaled * unit, axis=-1, keepdims=True)
    )


def shape_of(extent, dtype):
    return jax.ShapeDtypeStruct(extent, dtype)


def prepare_kernel(experts, ctxs, wide, where_ref, tokens_ref, weight_ref, small_ref, unit_ref, sent_ref, rows_ref):
    unit_ref[...] = normed(tokens_ref[...].astype(F32))[0].astype(BF16)
    gain = small_ref[:, experts + 1 : experts + 2].astype(F32)
    for k in range(3):
        scaled = (weight_ref[k].astype(F32) * gain).astype(BF16)
        for c in range(ctxs):
            piece = scaled[:, c * wide : (c + 1) * wide]
            sent_ref[c, :, k * wide : (k + 1) * wide] = piece
            rows_ref[:, (3 * c + k) * wide : (3 * c + k + 1) * wide] = piece
    for c in range(ctxs):
        sent_ref[c, :, 3 * wide :] = small_ref[...]


def prepare(tokens, weight_qkv, small, tp_rank, half, ctxs, wide, experts):
    _, rows, head_width = weight_qkv.shape
    width = tokens.shape[1]
    pad = small.shape[1]
    return pl.pallas_call(
        functools.partial(prepare_kernel, experts, ctxs, wide),
        name="prepare",
        out_shape=(
            shape_of((half, width), BF16),
            shape_of((ctxs, rows, 3 * wide + pad), BF16),
            shape_of((rows, 3 * head_width), BF16),
        ),
        grid_spec=pltpu.PrefetchScalarGridSpec(
            num_scalar_prefetch=1,
            grid=(1,),
            in_specs=[
                pl.BlockSpec((half, width), lambda i, w: (w[0], 0)),
                pl.BlockSpec(weight_qkv.shape, lambda i, w: (0, 0, 0)),
                pl.BlockSpec(small.shape, lambda i, w: (0, 0)),
            ],
            out_specs=[
                pl.BlockSpec((half, width), lambda i, w: (0, 0)),
                pl.BlockSpec((ctxs, rows, 3 * wide + pad), lambda i, w: (0, 0, 0)),
                pl.BlockSpec((rows, 3 * head_width), lambda i, w: (0, 0)),
            ],
        ),
    )(tp_rank, tokens, weight_qkv, small)


def middle_kernel(
    experts, tokens_ref, own_ref, par_ref, proj_own_ref, proj_par_ref, gain_ref, router_ref, route_ref,
    middle_ref, second_ref, probs_ref, gate_ref,
):
    branch = nt(own_ref[...], proj_own_ref[...]) + nt(par_ref[...], proj_par_ref[...])
    middle = tokens_ref[...].astype(F32) + branch
    middle_ref[...] = middle
    second = (normed(middle)[0] * gain_ref[...].astype(F32)).astype(BF16)
    second_ref[...] = second
    logits = nn(second, router_ref[...])
    lane = lax.broadcasted_iota(jnp.int32, logits.shape, 1)
    logits = jnp.where(lane < experts, logits, MASKED)
    powers = jnp.exp(logits - jnp.max(logits, axis=-1, keepdims=True))
    powers = jnp.where(lane < experts, powers, 0.0)
    probs = powers / jnp.sum(powers, axis=-1, keepdims=True)
    probs_ref[...] = probs
    gate_ref[...] = jnp.sum(jnp.where(lane == route_ref[...], probs, 0.0), axis=-1, keepdims=True)


ROWS = 256


def middle_step(tokens, own, par, proj_own, proj_par, gain, router, route, experts):
    count, width = tokens.shape
    features = own.shape[1]
    pad = router.shape[1]
    tile = min(ROWS, count)

    def rows(extent):
        return pl.BlockSpec((tile, extent), lambda i: (i, 0))

    def whole(array):
        return pl.BlockSpec(array.shape, lambda i: (0, 0))

    return pl.pallas_call(
        functools.partial(middle_kernel, experts),
        name="middle_step",
        grid=(count // tile,),
        out_shape=(
            shape_of((count, width), F32),
            shape_of((count, width), BF16),
            shape_of((count, pad), F32),
            shape_of((count, 1), F32),
        ),
        in_specs=[
            rows(width), rows(features), rows(features), whole(proj_own), whole(proj_par),
            whole(gain), whole(router), rows(1),
        ],
        out_specs=[rows(width), rows(width), rows(pad), rows(1)],
    )(tokens, own, par, proj_own, proj_par, gain, router, route)


def home_kernel(
    experts, limit, where_ref, cot_ref, middle_ref, second_ref, probs_ref, gate_ref, route_ref, target_ref,
    own_slot_ref, par_slot_ref, back_own_ref, back_par_ref, grad_ref, gain_ref, router_ref, proj_ref,
    output_ref, grad_middle_ref, grad_branch_ref, grad_mixed_ref, grad_logits_ref, grad_gain_ref,
):
    i = pl.program_id(0)
    tile, width = cot_ref.shape
    target = target_ref[...]
    pick_own = (target == own_slot_ref[...]).astype(F32).astype(BF16)
    pick_par = (target == par_slot_ref[...]).astype(F32).astype(BF16)
    fetched = nn(pick_own, back_own_ref[...]) + nn(pick_par, back_par_ref[...])
    grad_home = nn(pick_own, grad_ref[0]) + nn(pick_par, grad_ref[1])
    place = where_ref[0] + i * tile + lax.broadcasted_iota(jnp.int32, (tile, 1), 0)
    valid = (place < where_ref[1]).astype(F32)
    kept = (target < limit).astype(F32)
    gate = gate_ref[...]
    probs = probs_ref[...]
    middle = middle_ref[...]
    output_ref[...] = (valid * (middle + (kept * gate) * fetched)).astype(BF16)
    grad_out = valid * cot_ref[...].astype(F32)
    grad_gate = kept * jnp.sum(grad_out * fetched, axis=-1, keepdims=True)
    lane = lax.broadcasted_iota(jnp.int32, probs.shape, 1)
    hot = (lane == route_ref[...]).astype(F32)
    grad_logits = ((grad_gate * gate) * (hot - probs)).astype(BF16)
    grad_logits_ref[...] = grad_logits
    gain = gain_ref[...].astype(F32)
    unit, inverse = normed(middle)
    grad_second = grad_home + nt(grad_logits, router_ref[...])
    grad_gain = jnp.sum(grad_second * unit, axis=0, keepdims=True)

    @pl.when(i == 0)
    def _():
        grad_gain_ref[...] = grad_gain

    @pl.when(i > 0)
    def _():
        grad_gain_ref[...] += grad_gain

    grad_middle = grad_out + norm_back(grad_second * gain, unit, inverse)
    grad_middle_ref[...] = grad_middle
    grad_branch = grad_middle.astype(BF16)
    grad_branch_ref[...] = grad_branch
    grad_mixed_ref[...] = nn(grad_branch, proj_ref[...]).astype(BF16)


def home_step(
    cot, middle, second, probs, gate, route, target, own_slot, par_slot, back_own, back_par, grads,
    gain, router, proj, where, experts, limit,
):
    count, width = cot.shape
    features = proj.shape[1]
    pad = router.shape[1]
    tile = min(ROWS, count)

    def rows(extent):
        return pl.BlockSpec((tile, extent), lambda i, w: (i, 0))

    def whole(array):
        return pl.BlockSpec(array.shape, lambda i, w: (0,) * array.ndim)

    return pl.pallas_call(
        functools.partial(home_kernel, experts, limit),
        name="home_step",
        out_shape=(
            shape_of((count, width), BF16),
            shape_of((count, width), F32),
            shape_of((count, width), BF16),
            shape_of((count, features), BF16),
            shape_of((count, pad), BF16),
            shape_of((1, width), F32),
        ),
        grid_spec=pltpu.PrefetchScalarGridSpec(
            num_scalar_prefetch=1,
            grid=(count // tile,),
            in_specs=[
                rows(width), rows(width), rows(width), rows(pad), rows(1), rows(1), rows(1),
                whole(own_slot), whole(par_slot), whole(back_own), whole(back_par), whole(grads),
                whole(gain), whole(router), whole(proj),
            ],
            out_specs=[
                rows(width), rows(width), rows(width), rows(features), rows(pad),
                pl.BlockSpec((1, width), lambda i, w: (0, 0)),
            ],
        ),
    )(
        where, cot, middle, second, probs, gate, route, target, own_slot, par_slot, back_own, back_par,
        grads, gain, router, proj,
    )


def last_kernel(tokens_ref, grad_middle_ref, own_ref, par_ref, weight_own_ref, weight_par_ref, out_ref):
    ctxs, _, piece = own_ref.shape
    scaled = None
    for got, weight in ((own_ref, weight_own_ref), (par_ref, weight_par_ref)):
        for c in range(ctxs):
            part = nt(got[c], weight[:, c * piece : (c + 1) * piece])
            scaled = part if scaled is None else scaled + part
    unit, inverse = normed(tokens_ref[...].astype(F32))
    out_ref[...] = grad_middle_ref[...] + norm_back(scaled, unit, inverse)


def last_step(tokens, grad_middle, own, par, weight_own, weight_par):
    count, width = tokens.shape
    ctxs, _, piece = own.shape
    tile = min(ROWS, count)
    rows = pl.BlockSpec((tile, width), lambda i: (i, 0))
    got = pl.BlockSpec((ctxs, tile, piece), lambda i: (0, i, 0))
    weight = pl.BlockSpec(weight_own.shape, lambda i: (0, 0))
    return pl.pallas_call(
        last_kernel,
        name="last_step",
        grid=(count // tile,),
        out_shape=shape_of((count, width), F32),
        in_specs=[rows, rows, got, got, weight, weight],
        out_specs=rows,
    )(tokens, grad_middle, own, par, weight_own, weight_par)


def owner_kernel(shards, ctxs, wide, got_ref, weight_ref, gain_ref, grad_ref, sum_ref):
    gain = gain_ref[...].astype(F32)
    total = jnp.zeros((got_ref.shape[1], 1), F32)
    for c in range(ctxs):
        raw = got_ref[c].astype(F32)
        for s in range(1, shards):
            raw = raw + got_ref[s * ctxs + c].astype(F32)
        for k in range(3):
            piece = raw[:, k * wide : (k + 1) * wide]
            grad_ref[k, :, c * wide : (c + 1) * wide] = piece * gain
            weight = weight_ref[k, :, c * wide : (c + 1) * wide].astype(F32)
            total = total + jnp.sum(piece * weight, axis=-1, keepdims=True)
    sum_ref[...] = jnp.broadcast_to(total, sum_ref.shape)


def owner_step(got, weight_qkv, gain, shards, ctxs, wide):
    rows = weight_qkv.shape[1]
    return pl.pallas_call(
        functools.partial(owner_kernel, shards, ctxs, wide),
        name="owner_step",
        out_shape=(shape_of(weight_qkv.shape, F32), shape_of((rows, 128), F32)),
        in_specs=[pl.BlockSpec(memory_space=pltpu.VMEM)] * 3,
        out_specs=(pl.BlockSpec(memory_space=pltpu.VMEM),) * 2,
    )(got, weight_qkv, gain)


def local(
    sizes, tokens, lengths, routes, weight_qkv, weight_proj, router, gain_one, gain_two,
    w_in, w_out, cotangent,
):
    shards, ctxs, tps = sizes
    group = ("shard", "ctx")
    groups = shards * ctxs
    slots, count, width = tokens.shape
    assert slots == 1 and tps == 2
    head_width = weight_qkv.shape[2]
    wide = head_width // ctxs
    heads = wide // HEAD_DIM
    rows = weight_qkv.shape[1]
    experts = router.shape[1]
    capacity = max(2, (5 * count + 4 * experts - 1) // (4 * experts))
    assert capacity % 2 == 0
    half_cap = capacity // 2
    half = count // tps
    length_all = ctxs * count
    ctx_rank = lax.axis_index("ctx")
    tp_rank = lax.axis_index("tp")
    rows_in = tokens[0]
    cot = cotangent[0]

    pad = -(-(experts + 2) // 128) * 128
    small = jnp.concatenate(
        [router, gain_two[:, None], gain_one[:, None], jnp.zeros((rows, pad - experts - 2), BF16)],
        axis=1,
    )
    unit_half, sent_weights, row_weights = prepare(
        rows_in, weight_qkv, small, tp_rank.astype(jnp.int32)[None], half, ctxs, wide, experts
    )
    unit_all, got_weights = exchange(
        "gather_rows", 1, sizes,
        [
            Item(
                "ctx", unit_half, [shape_of((ctxs, tps, half, width), BF16)],
                lambda ref, p: ref,
                lambda ref, q, t: ref.at[q, t],
                relay=lambda ref, q, t: ref.at[q, t],
                block=(half, width),
            ),
            Item(
                "all", sent_weights, [shape_of((groups, rows, 3 * wide + pad), BF16)],
                lambda ref, p: ref.at[p % ctxs],
                lambda ref, q, t: ref.at[q],
                block=(rows, 3 * wide + pad),
            ),
        ],
    )
    unit_all, got_weights, row_weights, weight_late, routes, cot_late = lax.optimization_barrier(
        (unit_all, got_weights, row_weights, weight_proj, routes, cot)
    )
    whole_qkv = lax.all_gather(row_weights, group, axis=0, tiled=True)
    whole_proj = lax.all_gather(weight_late, group, axis=0, tiled=True)
    unit_all = unit_all.reshape(length_all, width)
    got_weights = got_weights.reshape(width, 3 * wide + pad)
    own_qkv = got_weights[:, : 3 * wide]
    full_small = got_weights[:, 3 * wide :]
    full_two = got_weights[:, 3 * wide + experts].reshape(1, width)

    places = ctx_rank * count + jnp.arange(count, dtype=jnp.int32)
    route = routes.reshape(count)
    valid = places < lengths[0]
    route_hot = route[:, None] == jnp.arange(experts, dtype=jnp.int32)[None, :]
    counted = (route_hot & valid[:, None]).astype(BF16)
    order = jnp.arange(count, dtype=jnp.int32)
    below = (order[:, None] > order[None, :]).astype(BF16)
    earlier = nn(below, counted)
    place = jnp.sum(earlier * counted.astype(F32), axis=1).astype(jnp.int32)
    kept = valid & (place < capacity)
    target = jnp.where(kept, route * capacity + place, experts * capacity)
    slot = jnp.arange(experts * half_cap, dtype=jnp.int32)
    slot = (slot // half_cap) * capacity + slot % half_cap
    own_slot = slot + tp_rank * half_cap
    par_slot = slot + (1 - tp_rank) * half_cap
    picked = own_slot[:, None] == target[None, :]
    pick_own = picked.astype(BF16)

    sent_cot = nn(pick_own, cot_late).astype(BF16).reshape(experts, half_cap, width)
    got_cot = lax.all_to_all(sent_cot, group, split_axis=0, concat_axis=0, tiled=True)

    projected = nn(unit_all, own_qkv).astype(BF16)
    mixed_heads, lse = attention_forward(projected, lengths, heads)

    def passed(array):
        return Item(
            "pair", array, [shape_of(array.shape, BF16)],
            lambda ref, p: ref, None, relay=lambda ref, q, t: ref, keep=False,
        )

    mixed_own, mixed_par, proj_par, qkv_par = exchange(
        "mixed_home", 2, sizes,
        [
            Item(
                "ctx", mixed_heads,
                [shape_of((count, head_width), BF16), shape_of((count, head_width), BF16)],
                lambda ref, p: ref.at[pl.ds(pl.multiple_of(p * count, count), count), :],
                lambda ref, q, t: ref.at[:, pl.ds(pl.multiple_of(q * wide, wide), wide)],
                relay=lambda ref, q, t: ref.at[:, pl.ds(pl.multiple_of(q * wide, wide), wide)],
                block=(count, wide),
            ),
            passed(whole_proj),
            passed(whole_qkv),
        ],
    )

    route_column = routes.reshape(count, 1)
    middle, second, probs, gate = middle_step(
        rows_in, mixed_own, mixed_par, whole_proj, proj_par, full_two, full_small, route_column, experts
    )
    sent_rows = nn(pick_own, second).astype(BF16).reshape(experts, half_cap, width)
    gate_rows = jnp.sum(jnp.where(picked, gate.reshape(1, count), 0.0), axis=1)
    gate_rows = gate_rows.reshape(experts, half_cap)
    lanes = -(-half_cap // 128) * 128
    gate_rows = jnp.broadcast_to(
        jnp.pad(gate_rows, ((0, 0), (0, lanes - half_cap)))[:, None, :], (experts, 8, lanes)
    )

    def scattered(array):
        block = array.shape[1:]
        return Item(
            "all", array, [shape_of((tps,) + array.shape, array.dtype)],
            lambda ref, p: ref.at[p],
            lambda ref, q, t: ref.at[0, q],
            relay=lambda ref, q, t: ref.at[1, q],
            block=block,
        )

    got_gates, got_rows, cot_par = exchange(
        "dispatch", 3, sizes, [scattered(gate_rows), scattered(sent_rows), passed(got_cot)]
    )

    slots_half = groups * half_cap
    total_rows = tps * slots_half
    arrived = got_rows.reshape(total_rows, width)
    gates = got_gates[:, :, 0, :half_cap].reshape(total_rows)
    cot_rows = jnp.concatenate([got_cot, cot_par], axis=0).reshape(total_rows, width)
    grad_rows = (gates[:, None] * cot_rows.astype(F32)).astype(BF16)
    pre = nn(arrived, w_in[0])
    hidden, gelu_back = jax.vjp(jax.nn.gelu, pre)
    hidden = hidden.astype(BF16)
    partial_out = nn(hidden, w_out[0]).astype(BF16).reshape(tps, groups, half_cap, width)
    summed = pair_sum("sum_out", 4, partial_out)
    going_back = lax.all_to_all(summed, group, split_axis=0, concat_axis=0, tiled=True)

    grad_hidden = nt(grad_rows, w_out[0])
    grad_pre = gelu_back(grad_hidden)[0].astype(BF16)
    partial_grad = nt(grad_pre, w_in[0]).astype(BF16).reshape(tps, groups, half_cap, width)
    grad_summed = pair_sum("sum_grad", 5, partial_grad)
    grad_home, back_par = exchange(
        "grad_home", 6, sizes, [scattered(grad_summed), passed(going_back)]
    )

    where = jnp.stack([ctx_rank * count, lengths[0]]).astype(jnp.int32)
    output, grad_middle, grad_branch, grad_mixed_own, grad_logits, grad_gain_two = home_step(
        cot, middle, second, probs, gate, route_column, target.reshape(count, 1),
        own_slot.reshape(1, slots_half), par_slot.reshape(1, slots_half),
        going_back.reshape(slots_half, width), back_par.reshape(slots_half, width),
        grad_home.reshape(tps, slots_half, width), full_two, full_small, whole_proj, where, experts,
        experts * capacity,
    )
    output = output.reshape(slots, count, width)

    (grad_mixed,) = exchange(
        "grad_mixed", 7, sizes,
        [
            Item(
                "ctx", grad_mixed_own, [shape_of((length_all, wide), BF16)],
                lambda ref, p: ref.at[:, pl.ds(pl.multiple_of(p * wide, wide), wide)],
                lambda ref, q, t: ref.at[pl.ds(pl.multiple_of(q * count, count), count), :],
                block=(count, wide),
            ),
        ],
    )
    grad_router = tn(second, grad_logits)[:, :experts]
    grad_proj = tn(grad_branch, mixed_own)
    packed = jnp.concatenate(
        [
            grad_proj, grad_router, grad_gain_two.reshape(width, 1),
            jnp.zeros((width, pad - experts - 1), F32),
        ],
        axis=1,
    )
    owned = lax.psum_scatter(packed, group, scatter_dimension=0, tiled=True)
    owned_proj = owned[:, :head_width]
    owned_router = owned[:, head_width : head_width + experts]
    owned_two = owned[:, head_width + experts]

    grad_projected = attention_backward(projected, mixed_heads, grad_mixed, lse, lengths, heads)
    grad_own = lax.all_to_all(
        grad_projected.reshape(ctxs, count, 3 * wide), "ctx", split_axis=0, concat_axis=0, tiled=True
    )

    unit_late, hidden, arrived, grad_rows, grad_pre, grad_projected = lax.optimization_barrier(
        (unit_all, hidden, arrived, grad_rows, grad_pre, grad_projected)
    )
    grad_weight = tn(unit_late, grad_projected).astype(BF16).reshape(groups, rows, 3 * wide)
    got_grad = lax.all_to_all(grad_weight, group, split_axis=0, concat_axis=0, tiled=True)
    grad_w_out = tn(hidden, grad_rows)[None]
    grad_w_in = tn(arrived, grad_pre)[None]

    (grad_par,) = exchange("grad_pair", 8, sizes, [passed(grad_own)])
    grad_tokens = last_step(rows_in, grad_middle, grad_own, grad_par, whole_qkv, qkv_par)
    grad_tokens = grad_tokens.reshape(slots, count, width)
    owned_qkv, sums = owner_step(got_grad, weight_qkv, gain_one.reshape(rows, 1), shards, ctxs, wide)
    owned_one = lax.psum(sums[:, 0], "tp")
    return (
        output,
        grad_tokens,
        owned_qkv,
        owned_proj,
        owned_router,
        owned_one,
        owned_two,
        grad_w_in,
        grad_w_out,
    )


def solution(mesh):
    sizes = (mesh.shape["shard"], mesh.shape["ctx"], mesh.shape["tp"])
    return jax.shard_map(
        functools.partial(local, sizes),
        mesh=mesh,
        in_specs=(
            P("shard", "ctx", None),
            P("shard"),
            P("shard", "ctx", None),
            P(None, ("shard", "ctx"), "tp"),
            P(("shard", "ctx"), "tp"),
            P(("shard", "ctx"), None),
            P(("shard", "ctx")),
            P(("shard", "ctx")),
            P(("shard", "ctx"), None, "tp"),
            P(("shard", "ctx"), "tp", None),
            P("shard", "ctx", None),
        ),
        out_specs=(
            P("shard", "ctx", None),
            P("shard", "ctx", None),
            P(None, ("shard", "ctx"), "tp"),
            P(("shard", "ctx"), "tp"),
            P(("shard", "ctx"), None),
            P(("shard", "ctx")),
            P(("shard", "ctx")),
            P(("shard", "ctx"), None, "tp"),
            P(("shard", "ctx"), "tp", None),
        ),
        check_vma=False,
    )
```

```python
import functools

import jax
import jax.numpy as jnp
from jax import lax
from jax.experimental import pallas as pl
from jax.experimental.pallas import tpu as pltpu
from jax.sharding import PartitionSpec as P

HEAD_DIM = 64
EPSILON = 1e-05
MASKED = -1e30
LOG2E = 1.4426950408889634
BLOCK = 512
GELU_A = 0.7978845608028654
GELU_B = 0.044715
MESH = pl.DeviceIdType.MESH
BF16 = jnp.bfloat16
F32 = jnp.float32


class Item:
    def __init__(self, group, ins, outs, src, dst, relay=None, block=None, keep=True):
        self.group, self.ins, self.outs = group, ins, outs
        self.src, self.dst, self.relay, self.block, self.keep = src, dst, relay, block, keep


def exchange(collective_id, sizes, items):
    shards, ctxs, tps = sizes
    count_all = shards * ctxs
    operands = [item.ins for item in items]
    out_shapes = [shape for item in items for shape in item.outs]
    scratch = []
    for item in items:
        n = {"ctx": ctxs, "all": count_all, "pair": 1}[item.group]
        item.n = n
        scratch += [pltpu.SemaphoreType.DMA((n,)) for _ in range(4)]
        scratch.append(pltpu.SemaphoreType.DMA((2,)))
        if item.keep:
            scratch.append(pltpu.VMEM(item.block, item.ins.dtype))
    wide = any(item.group == "all" for item in items)
    near = any(item.group == "ctx" for item in items)
    paired = any(item.group == "pair" or item.relay is not None for item in items)

    def body(*refs):
        in_refs = refs[: len(operands)]
        out_refs = refs[len(operands) : len(operands) + len(out_shapes)]
        rest = list(refs[len(operands) + len(out_shapes) :])
        me_s, me_c, me_t = lax.axis_index("shard"), lax.axis_index("ctx"), lax.axis_index("tp")
        me_all = me_s * ctxs + me_c
        other = tps - 1 - me_t
        partner = {"tp": other}

        def place(group, p):
            if group == "ctx":
                return {"ctx": p}
            return {"shard": p // ctxs, "ctx": p % ctxs}

        barrier = pltpu.get_barrier_semaphore()
        group, size, me = ("all", count_all, me_all) if wide else ("ctx", ctxs, me_c)
        greeted = 0
        if wide or near:

            def greet(k, carry):
                peer = lax.rem(me + k, size)
                pl.semaphore_signal(
                    barrier, inc=1, device_id=place(group, peer), device_id_type=MESH
                )
                return carry

            lax.fori_loop(1, size, greet, 0)
            greeted += size - 1
        if paired:
            pl.semaphore_signal(barrier, inc=1, device_id=partner, device_id_type=MESH)
            greeted += 1
        pl.semaphore_wait(barrier, greeted)

        jobs = []
        at = 0
        for item, source in zip(items, in_refs):
            outs = out_refs[at : at + len(item.outs)]
            at += len(item.outs)
            sems = [rest.pop(0) for _ in range(5)]
            stage = rest.pop(0) if item.keep else None
            jobs.append((item, source, outs, sems, stage))

        def make(item, source, outs, sems, k, peer, sender):
            return pltpu.make_async_remote_copy(
                src_ref=item.src(source, peer),
                dst_ref=item.dst(outs[0], sender, me_t),
                send_sem=sems[0].at[k],
                recv_sem=sems[1].at[sender],
                device_id=place(item.group, peer),
                device_id_type=MESH,
            )

        def make_relay(item, source, outs, sems, k, member, first):
            mine = {"ctx": me_c, "all": me_all, "pair": 0}[item.group]
            return pltpu.make_async_remote_copy(
                src_ref=item.src(source, mine) if first else item.dst(outs[0], member, me_t),
                dst_ref=item.relay(outs[-1], member, me_t),
                send_sem=sems[2].at[k],
                recv_sem=sems[3].at[member],
                device_id=partner,
                device_id_type=MESH,
            )

        def each(n, act):
            def step(k, carry):
                act(k)
                return carry

            lax.fori_loop(1, n, step, 0)

        mine_of = {"ctx": me_c, "all": me_all, "pair": 0}
        for item, source, outs, sems, stage in jobs:
            mine = mine_of[item.group]
            if item.n > 1:

                def send(k, item=item, source=source, outs=outs, sems=sems, mine=mine):
                    peer = lax.rem(mine + k, item.n)
                    make(item, source, outs, sems, k, peer, mine).start()

                each(item.n, send)
            if item.relay is not None:
                make_relay(item, source, outs, sems, 0, mine, True).start()
        for item, source, outs, sems, stage in jobs:
            if item.keep:
                pltpu.make_async_copy(
                    item.src(source, mine_of[item.group]), stage, sems[4].at[0]
                ).start()
        for item, source, outs, sems, stage in jobs:
            if item.keep:
                mine = mine_of[item.group]
                pltpu.make_async_copy(item.src(source, mine), stage, sems[4].at[0]).wait()
                pltpu.make_async_copy(
                    stage, item.dst(outs[0], mine, me_t), sems[4].at[1]
                ).start()
        for item, source, outs, sems, stage in jobs:
            mine = mine_of[item.group]
            if item.n > 1:

                def take(k, item=item, source=source, outs=outs, sems=sems, mine=mine):
                    member = lax.rem(mine + item.n - k, item.n)
                    peer = lax.rem(mine + k, item.n)
                    make(item, source, outs, sems, k, peer, member).wait_recv()
                    if item.relay is not None:
                        make_relay(item, source, outs, sems, k, member, False).start()

                each(item.n, take)
        for item, source, outs, sems, stage in jobs:
            mine = mine_of[item.group]
            if item.n > 1:

                def sent(k, item=item, source=source, outs=outs, sems=sems, mine=mine):
                    peer = lax.rem(mine + k, item.n)
                    make(item, source, outs, sems, k, peer, mine).wait_send()

                each(item.n, sent)
            if item.relay is not None:
                make_relay(item, source, outs, sems, 0, mine, True).wait()
                if item.n > 1:

                    def passed(k, item=item, source=source, outs=outs, sems=sems, mine=mine):
                        member = lax.rem(mine + item.n - k, item.n)
                        make_relay(item, source, outs, sems, k, member, False).wait()

                    each(item.n, passed)
            if item.keep:
                pltpu.make_async_copy(
                    stage, item.dst(outs[0], mine, me_t), sems[4].at[1]
                ).wait()

    anywhere = pl.BlockSpec(memory_space=pl.ANY)
    return pl.pallas_call(
        body,
        out_shape=tuple(out_shapes),
        in_specs=[anywhere] * len(operands),
        out_specs=tuple([anywhere] * len(out_shapes)),
        scratch_shapes=scratch,
        compiler_params=pltpu.CompilerParams(collective_id=collective_id, has_side_effects=True),
    )(*operands)


def gather_step(collective_id, sizes, unit_half, weights):
    shards, ctxs, tps = sizes
    groups = shards * ctxs
    assert ctxs == 4 and tps == 2
    half, width = unit_half.shape
    part = half // 2
    piece = weights.shape[1:]

    def body(rows_ref, weights_ref, all_ref, got_ref, rows_stage, weights_stage, send, take, relay, taken, put, away, home):
        me_s, me_c, me_t = lax.axis_index("shard"), lax.axis_index("ctx"), lax.axis_index("tp")
        me = me_s * ctxs + me_c
        low = me_c % 2
        high = me_c // 2
        near = high * 2 + (1 - low)
        side = (1 - high) * 2 + low
        far = (1 - high) * 2 + (1 - low)
        partner = {"tp": 1 - me_t}

        def place(p):
            return {"shard": p // ctxs, "ctx": p % ctxs}

        barrier = pltpu.get_barrier_semaphore()

        def greet(k, carry):
            pl.semaphore_signal(
                barrier, inc=1, device_id=place(lax.rem(me + k, groups)), device_id_type=MESH
            )
            return carry

        lax.fori_loop(1, groups, greet, 0)
        pl.semaphore_signal(barrier, inc=1, device_id=partner, device_id_type=MESH)
        pl.semaphore_wait(barrier, groups)

        def copy(src, dst, src_sem, dst_sem, device):
            return pltpu.make_async_remote_copy(
                src_ref=src, dst_ref=dst, send_sem=src_sem, recv_sem=dst_sem,
                device_id=device, device_id_type=MESH,
            )

        def rows_of(p):
            return rows_ref.at[pl.ds(p * part, part), :]

        def slot(q, p):
            return all_ref.at[q, me_t, pl.ds(p * part, part), :]

        to_near = [copy(rows_of(p), slot(me_c, p), send.at[p], take.at[p], {"ctx": near}) for p in (0, 1)]
        to_side = [
            copy(rows_of(1 - p), slot(me_c, 1 - p), send.at[2 + p], take.at[2 + p], {"ctx": side})
            for p in (0, 1)
        ]
        for p in (0, 1):
            to_near[p].start()
            to_side[p].start()
        mine = copy(rows_ref, all_ref.at[me_c, me_t], relay.at[6], taken.at[6], partner)
        mine.start()

        def weights_to(k, carry):
            peer = lax.rem(me + k, groups)
            copy(
                weights_ref.at[peer % ctxs], got_ref.at[me], put.at[k], away.at[me], place(peer)
            ).start()
            return carry

        lax.fori_loop(1, groups, weights_to, 0)
        stays = [
            pltpu.make_async_copy(rows_ref, rows_stage, home.at[0]),
            pltpu.make_async_copy(weights_ref.at[me_c], weights_stage, home.at[1]),
        ]
        lands = [
            pltpu.make_async_copy(rows_stage, all_ref.at[me_c, me_t], home.at[2]),
            pltpu.make_async_copy(weights_stage, got_ref.at[me], home.at[3]),
        ]
        for stay in stays:
            stay.start()
        for stay, land in zip(stays, lands):
            stay.wait()
            land.start()

        got = [slot(near, 0), slot(near, 1), slot(side, 1), slot(side, 0), slot(far, 0), slot(far, 1)]
        relays = [copy(ref, ref, relay.at[n], taken.at[n], partner) for n, ref in enumerate(got)]
        on_side = copy(got[0], got[0], send.at[4], take.at[4], {"ctx": side})
        on_near = copy(got[2], got[2], send.at[5], take.at[5], {"ctx": near})
        to_near[0].wait_recv()
        on_side.start()
        relays[0].start()
        to_side[0].wait_recv()
        on_near.start()
        relays[2].start()
        to_near[1].wait_recv()
        relays[1].start()
        to_side[1].wait_recv()
        relays[3].start()
        from_side = copy(got[4], got[4], send.at[4], take.at[4], {"ctx": side})
        from_near = copy(got[5], got[5], send.at[5], take.at[5], {"ctx": near})
        from_side.wait_recv()
        relays[4].start()
        from_near.wait_recv()
        relays[5].start()

        def weights_from(k, carry):
            member = lax.rem(me + groups - k, groups)
            copy(
                weights_ref.at[0], got_ref.at[member], put.at[k], away.at[member], place(member)
            ).wait_recv()
            return carry

        lax.fori_loop(1, groups, weights_from, 0)

        def weights_sent(k, carry):
            peer = lax.rem(me + k, groups)
            copy(
                weights_ref.at[peer % ctxs], got_ref.at[me], put.at[k], away.at[me], place(peer)
            ).wait_send()
            return carry

        lax.fori_loop(1, groups, weights_sent, 0)
        for p in (0, 1):
            to_near[p].wait_send()
            to_side[p].wait_send()
        on_side.wait_send()
        on_near.wait_send()
        mine.wait()
        for passing in relays:
            passing.wait()
        for land in lands:
            land.wait()

    anywhere = pl.BlockSpec(memory_space=pl.ANY)
    return pl.pallas_call(
        body,
        name="gather_rows",
        out_shape=(
            jax.ShapeDtypeStruct((ctxs, tps, half, width), BF16),
            jax.ShapeDtypeStruct((groups,) + piece, BF16),
        ),
        in_specs=[anywhere] * 2,
        out_specs=(anywhere, anywhere),
        scratch_shapes=[
            pltpu.VMEM((half, width), BF16),
            pltpu.VMEM(piece, BF16),
            pltpu.SemaphoreType.DMA((6,)),
            pltpu.SemaphoreType.DMA((6,)),
            pltpu.SemaphoreType.DMA((7,)),
            pltpu.SemaphoreType.DMA((7,)),
            pltpu.SemaphoreType.DMA((groups,)),
            pltpu.SemaphoreType.DMA((groups,)),
            pltpu.SemaphoreType.DMA((4,)),
        ],
        compiler_params=pltpu.CompilerParams(collective_id=collective_id, has_side_effects=True),
    )(unit_half, weights)


def nt(left, right):
    return lax.dot_general(left, right, (((1,), (1,)), ((), ())), preferred_element_type=F32)


def nn(left, right):
    return lax.dot_general(left, right, (((1,), (0,)), ((), ())), preferred_element_type=F32)


def tn(left, right):
    return lax.dot_general(left, right, (((0,), (0,)), ((), ())), preferred_element_type=F32)


def stacked(rows, heads):
    lane = lax.broadcasted_iota(jnp.int32, rows.shape, 1) // HEAD_DIM
    return jnp.concatenate([jnp.where(lane == h, rows, jnp.zeros_like(rows)) for h in range(heads)], 0)


def merged(pieces, heads):
    block = pieces.shape[0] // heads
    lane = lax.broadcasted_iota(jnp.int32, (block, pieces.shape[1]), 1) // HEAD_DIM
    total = pieces[:block]
    for h in range(1, heads):
        total = jnp.where(lane == h, pieces[h * block : (h + 1) * block], total)
    return total


def forward_kernel(heads, size, span, spans, len_ref, q_ref, k_ref, v_ref, o_ref, lse_ref, turned):
    i = pl.program_id(0)
    length = len_ref[0]
    scale = HEAD_DIM ** (-0.5)
    tall = heads * size
    wide = heads * HEAD_DIM

    @pl.when(i == 0)
    def _():
        def turn(j, carry):
            place = pl.ds(pl.multiple_of(j * span, span), span)
            turned[j] = jnp.transpose(v_ref[place, :].astype(F32)).astype(BF16)
            return carry

        lax.fori_loop(0, spans, turn, 0)

    queries = stacked((q_ref[...].astype(F32) * scale).astype(BF16), heads)
    inner = lax.broadcasted_iota(jnp.int32, (1, tall), 1) % size
    limit = jnp.minimum(i * size + inner, length - 1)
    full = (jnp.minimum(i * size, length - 1) + 1) // span
    every = (jnp.minimum((i + 1) * size, length) + span - 1) // span

    def step(masked, j, state):
        top, total, accum = state
        place = pl.ds(pl.multiple_of(j * span, span), span)
        scores = nt(k_ref[place, :], queries) * LOG2E
        if masked:
            column = j * span + lax.broadcasted_iota(jnp.int32, (span, tall), 0)
            scores = jnp.where(column <= limit, scores, MASKED)
        new_top = jnp.maximum(top, jnp.max(scores, axis=0, keepdims=True))
        factor = jnp.exp2(top - new_top)
        weights = jnp.exp2(scores - new_top)
        total = total * factor + jnp.sum(weights, axis=0, keepdims=True)
        accum = accum * factor + nn(turned[j], weights.astype(BF16))
        return new_top, total, accum

    state = (
        jnp.full((1, tall), MASKED, F32),
        jnp.zeros((1, tall), F32),
        jnp.zeros((wide, tall), F32),
    )
    state = lax.fori_loop(0, full, functools.partial(step, False), state)
    top, total, accum = lax.fori_loop(full, every, functools.partial(step, True), state)
    o_ref[...] = merged(jnp.transpose(accum / total), heads).astype(BF16)
    lse_ref[0] = top + jnp.log2(total)


def attention_forward(projected, lengths, heads):
    count, _ = projected.shape
    wide = heads * HEAD_DIM
    size = BLOCK
    span = 2 * BLOCK
    blocks = count // size
    return pl.pallas_call(
        functools.partial(forward_kernel, heads, size, span, count // span),
        name="attention_forward",
        out_shape=(
            jax.ShapeDtypeStruct((count, wide), BF16),
            jax.ShapeDtypeStruct((blocks, 1, heads * size), F32),
        ),
        grid_spec=pltpu.PrefetchScalarGridSpec(
            num_scalar_prefetch=1,
            grid=(blocks,),
            in_specs=[
                pl.BlockSpec((size, wide), lambda i, n: (i, 0)),
                pl.BlockSpec((count, wide), lambda i, n: (0, 1)),
                pl.BlockSpec((count, wide), lambda i, n: (0, 2)),
            ],
            out_specs=[
                pl.BlockSpec((size, wide), lambda i, n: (i, 0)),
                pl.BlockSpec((1, 1, heads * size), lambda i, n: (i, 0, 0)),
            ],
            scratch_shapes=[pltpu.VMEM((count // span, wide, span), BF16)],
        ),
        cost_estimate=pl.CostEstimate(
            flops=16 * count * count * wide,
            bytes_accessed=8 * count * wide,
            transcendentals=heads * count * count // 2,
        ),
    )(lengths, projected, projected, projected)


def backward_kernel(
    heads, size, blocks, len_ref, q_ref, k_ref, v_ref, o_ref, do_ref, lse_ref, out_ref,
    queries, grads, delta, grad_queries,
):
    j = pl.program_id(0)
    length = len_ref[0]
    scale = HEAD_DIM ** (-0.5)
    tall = heads * size
    wide = heads * HEAD_DIM

    @pl.when(j == 0)
    def _():
        def prepare(i, carry):
            place = pl.ds(pl.multiple_of(i * size, size), size)
            tall_place = pl.ds(pl.multiple_of(i * tall, tall), tall)
            queries[tall_place, :] = stacked((q_ref[place, :].astype(F32) * scale).astype(BF16), heads)
            grad = do_ref[place, :]
            grads[tall_place, :] = stacked(grad, heads)
            product = jnp.transpose(grad.astype(F32) * o_ref[place, :].astype(F32))
            delta[i] = jnp.concatenate(
                [
                    jnp.sum(product[h * HEAD_DIM : (h + 1) * HEAD_DIM], axis=0, keepdims=True)
                    for h in range(heads)
                ],
                axis=1,
            )
            grad_queries[i] = jnp.zeros((wide, tall), F32)
            return carry

        lax.fori_loop(0, blocks, prepare, 0)

    keys = k_ref[...]
    values = v_ref[...]
    keys_turned = jnp.transpose(keys.astype(F32)).astype(BF16)
    column = j * size + lax.broadcasted_iota(jnp.int32, (size, tall), 0)
    inner = lax.broadcasted_iota(jnp.int32, (1, tall), 1) % size

    def step(masked, i, state):
        grad_keys, grad_values = state
        tall_place = pl.ds(pl.multiple_of(i * tall, tall), tall)
        query = queries[tall_place, :]
        grad = grads[tall_place, :]
        power = nt(keys, query) * LOG2E - lse_ref[i]
        if masked:
            limit = jnp.minimum(i * size + inner, length - 1)
            power = jnp.where(column <= limit, power, MASKED)
        weights = jnp.exp2(power)
        grad_values = grad_values + nn(weights.astype(BF16), grad)
        grad_scores = (weights * (nt(values, grad) - delta[i])).astype(BF16)
        grad_keys = grad_keys + nn(grad_scores, query)
        grad_queries[i] += nn(keys_turned, grad_scores)
        return grad_keys, grad_values

    state = (jnp.zeros((size, wide), F32), jnp.zeros((size, wide), F32))
    crosses = (j + 1) * size > length
    begin = jnp.where(j * size < length, j, blocks)
    middle = jnp.where(crosses, blocks, j + 1)
    state = lax.fori_loop(begin, middle, functools.partial(step, True), state)
    grad_keys, grad_values = lax.fori_loop(middle, blocks, functools.partial(step, False), state)
    place = pl.ds(pl.multiple_of(j * size, size), size)
    out_ref[place, wide : 2 * wide] = grad_keys.astype(BF16)
    out_ref[place, 2 * wide : 3 * wide] = grad_values.astype(BF16)

    @pl.when(j == blocks - 1)
    def _():
        def finish(i, carry):
            block_place = pl.ds(pl.multiple_of(i * size, size), size)
            turned = jnp.transpose(grad_queries[i])
            out_ref[block_place, :wide] = (merged(turned, heads) * scale).astype(BF16)
            return carry

        lax.fori_loop(0, blocks, finish, 0)


def attention_backward(projected, mixed, grad_mixed, lse, lengths, heads):
    count, _ = projected.shape
    wide = heads * HEAD_DIM
    size = BLOCK
    blocks = count // size
    tall = heads * size
    return pl.pallas_call(
        functools.partial(backward_kernel, heads, size, blocks),
        name="attention_backward",
        out_shape=jax.ShapeDtypeStruct((count, 3 * wide), BF16),
        grid_spec=pltpu.PrefetchScalarGridSpec(
            num_scalar_prefetch=1,
            grid=(blocks,),
            in_specs=[
                pl.BlockSpec((count, wide), lambda j, n: (0, 0)),
                pl.BlockSpec((size, wide), lambda j, n: (j, 1)),
                pl.BlockSpec((size, wide), lambda j, n: (j, 2)),
                pl.BlockSpec((count, wide), lambda j, n: (0, 0)),
                pl.BlockSpec((count, wide), lambda j, n: (0, 0)),
                pl.BlockSpec((blocks, 1, tall), lambda j, n: (0, 0, 0)),
            ],
            out_specs=pl.BlockSpec((count, 3 * wide), lambda j, n: (0, 0)),
            scratch_shapes=[
                pltpu.VMEM((heads * count, wide), BF16),
                pltpu.VMEM((heads * count, wide), BF16),
                pltpu.VMEM((blocks, 1, tall), F32),
                pltpu.VMEM((blocks, wide, tall), F32),
            ],
        ),
        cost_estimate=pl.CostEstimate(
            flops=40 * count * count * wide,
            bytes_accessed=16 * count * wide,
            transcendentals=heads * count * count // 2,
        ),
    )(lengths, projected, projected, projected, mixed, grad_mixed, lse)


def pair_sum(collective_id, partial):
    shape = partial.shape[1:]

    def body(in_ref, out_ref, own, got, sems):
        other = {"tp": 1 - lax.axis_index("tp")}
        barrier = pltpu.get_barrier_semaphore()
        pl.semaphore_signal(barrier, inc=1, device_id=other, device_id_type=MESH)
        pl.semaphore_wait(barrier, 1)
        away = pltpu.make_async_remote_copy(
            src_ref=in_ref.at[1],
            dst_ref=got,
            send_sem=sems.at[0],
            recv_sem=sems.at[1],
            device_id=other,
            device_id_type=MESH,
        )
        away.start()
        here = pltpu.make_async_copy(in_ref.at[0], own, sems.at[2])
        here.start()
        here.wait()
        away.wait()

        def add(e, carry):
            out_ref[e] = (own[e].astype(F32) + got[e].astype(F32)).astype(BF16)
            return carry

        lax.fori_loop(0, shape[0], add, 0)

    return pl.pallas_call(
        body,
        out_shape=jax.ShapeDtypeStruct(shape, BF16),
        in_specs=[pl.BlockSpec(memory_space=pl.ANY)],
        out_specs=pl.BlockSpec(memory_space=pltpu.VMEM),
        scratch_shapes=[
            pltpu.VMEM(shape, BF16),
            pltpu.VMEM(shape, BF16),
            pltpu.SemaphoreType.DMA((3,)),
        ],
        compiler_params=pltpu.CompilerParams(collective_id=collective_id, has_side_effects=True),
    )(partial)


def normed(values):
    center = values - jnp.mean(values, axis=-1, keepdims=True)
    inverse = lax.rsqrt(jnp.mean(center * center, axis=-1, keepdims=True) + EPSILON)
    return center * inverse, inverse


def norm_back(scaled, unit, inverse):
    return inverse * (
        scaled
        - jnp.mean(scaled, axis=-1, keepdims=True)
        - unit * jnp.mean(scaled * unit, axis=-1, keepdims=True)
    )


def shape_of(extent, dtype):
    return jax.ShapeDtypeStruct(extent, dtype)


def prepare_kernel(experts, ctxs, wide, where_ref, tokens_ref, weight_ref, small_ref, unit_ref, sent_ref, rows_ref):
    unit_ref[...] = normed(tokens_ref[...].astype(F32))[0].astype(BF16)
    gain = small_ref[:, experts + 1 : experts + 2].astype(F32)
    for k in range(3):
        scaled = (weight_ref[k].astype(F32) * gain).astype(BF16)
        for c in range(ctxs):
            piece = scaled[:, c * wide : (c + 1) * wide]
            sent_ref[c, :, k * wide : (k + 1) * wide] = piece
            rows_ref[:, (3 * c + k) * wide : (3 * c + k + 1) * wide] = piece
    for c in range(ctxs):
        sent_ref[c, :, 3 * wide :] = small_ref[...]


def prepare(tokens, weight_qkv, small, tp_rank, half, ctxs, wide, experts):
    _, rows, head_width = weight_qkv.shape
    width = tokens.shape[1]
    pad = small.shape[1]
    return pl.pallas_call(
        functools.partial(prepare_kernel, experts, ctxs, wide),
        name="prepare",
        out_shape=(
            shape_of((half, width), BF16),
            shape_of((ctxs, rows, 3 * wide + pad), BF16),
            shape_of((rows, 3 * head_width), BF16),
        ),
        grid_spec=pltpu.PrefetchScalarGridSpec(
            num_scalar_prefetch=1,
            grid=(1,),
            in_specs=[
                pl.BlockSpec((half, width), lambda i, w: (w[0], 0)),
                pl.BlockSpec(weight_qkv.shape, lambda i, w: (0, 0, 0)),
                pl.BlockSpec(small.shape, lambda i, w: (0, 0)),
            ],
            out_specs=[
                pl.BlockSpec((half, width), lambda i, w: (0, 0)),
                pl.BlockSpec((ctxs, rows, 3 * wide + pad), lambda i, w: (0, 0, 0)),
                pl.BlockSpec((rows, 3 * head_width), lambda i, w: (0, 0)),
            ],
        ),
    )(tp_rank, tokens, weight_qkv, small)


def middle_kernel(
    experts, tokens_ref, own_ref, par_ref, proj_own_ref, proj_par_ref, gain_ref, router_ref, route_ref,
    middle_ref, second_ref, probs_ref, gate_ref,
):
    branch = nt(own_ref[...], proj_own_ref[...]) + nt(par_ref[...], proj_par_ref[...])
    middle = tokens_ref[...].astype(F32) + branch
    middle_ref[...] = middle
    second = (normed(middle)[0] * gain_ref[...].astype(F32)).astype(BF16)
    second_ref[...] = second
    logits = nn(second, router_ref[...])
    lane = lax.broadcasted_iota(jnp.int32, logits.shape, 1)
    logits = jnp.where(lane < experts, logits, MASKED)
    powers = jnp.exp(logits - jnp.max(logits, axis=-1, keepdims=True))
    powers = jnp.where(lane < experts, powers, 0.0)
    probs = powers / jnp.sum(powers, axis=-1, keepdims=True)
    probs_ref[...] = probs
    gate_ref[...] = jnp.sum(jnp.where(lane == route_ref[...], probs, 0.0), axis=-1, keepdims=True)


ROWS = 256


def middle_step(tokens, own, par, proj_own, proj_par, gain, router, route, experts):
    count, width = tokens.shape
    features = own.shape[1]
    pad = router.shape[1]
    tile = min(ROWS, count)

    def rows(extent):
        return pl.BlockSpec((tile, extent), lambda i: (i, 0))

    def whole(array):
        return pl.BlockSpec(array.shape, lambda i: (0, 0))

    return pl.pallas_call(
        functools.partial(middle_kernel, experts),
        name="middle_step",
        grid=(count // tile,),
        out_shape=(
            shape_of((count, width), F32),
            shape_of((count, width), BF16),
            shape_of((count, pad), F32),
            shape_of((count, 1), F32),
        ),
        in_specs=[
            rows(width), rows(features), rows(features), whole(proj_own), whole(proj_par),
            whole(gain), whole(router), rows(1),
        ],
        out_specs=[rows(width), rows(width), rows(pad), rows(1)],
    )(tokens, own, par, proj_own, proj_par, gain, router, route)


def home_kernel(
    limit, where_ref, cot_ref, middle_ref, second_ref, probs_ref, gate_ref, route_ref, target_ref,
    own_slot_ref, par_slot_ref, back_own_ref, back_par_ref, grad_ref, gain_ref, router_ref, proj_ref,
    output_ref, grad_middle_ref, grad_branch_ref, grad_mixed_ref, grad_logits_ref, grad_gain_ref,
):
    i = pl.program_id(0)
    tile, _ = cot_ref.shape
    target = target_ref[...]
    pick_own = (target == own_slot_ref[...]).astype(F32).astype(BF16)
    pick_par = (target == par_slot_ref[...]).astype(F32).astype(BF16)
    fetched = nn(pick_own, back_own_ref[...]) + nn(pick_par, back_par_ref[...])
    grad_home = nn(pick_own, grad_ref[0]) + nn(pick_par, grad_ref[1])
    place = where_ref[0] + i * tile + lax.broadcasted_iota(jnp.int32, (tile, 1), 0)
    valid = (place < where_ref[1]).astype(F32)
    kept = (target < limit).astype(F32)
    gate = gate_ref[...]
    probs = probs_ref[...]
    middle = middle_ref[...]
    output_ref[...] = (valid * (middle + (kept * gate) * fetched)).astype(BF16)
    grad_out = valid * cot_ref[...].astype(F32)
    grad_gate = kept * jnp.sum(grad_out * fetched, axis=-1, keepdims=True)
    lane = lax.broadcasted_iota(jnp.int32, probs.shape, 1)
    hot = (lane == route_ref[...]).astype(F32)
    grad_logits = ((grad_gate * gate) * (hot - probs)).astype(BF16)
    grad_logits_ref[...] = grad_logits
    gain = gain_ref[...].astype(F32)
    unit, inverse = normed(middle)
    grad_second = grad_home + nt(grad_logits, router_ref[...])
    grad_gain = jnp.sum(grad_second * unit, axis=0, keepdims=True)

    @pl.when(i == 0)
    def _():
        grad_gain_ref[...] = grad_gain

    @pl.when(i > 0)
    def _():
        grad_gain_ref[...] += grad_gain

    grad_middle = grad_out + norm_back(grad_second * gain, unit, inverse)
    grad_middle_ref[...] = grad_middle
    grad_branch = grad_middle.astype(BF16)
    grad_branch_ref[...] = grad_branch
    grad_mixed = nn(grad_branch, proj_ref[...]).astype(BF16)
    ctxs, _, wide = grad_mixed_ref.shape
    for c in range(ctxs):
        grad_mixed_ref[c] = grad_mixed[:, c * wide : (c + 1) * wide]


def home_step(
    cot, middle, second, probs, gate, route, target, own_slot, par_slot, back_own, back_par, grads,
    gain, router, proj, where, limit, ctxs,
):
    count, width = cot.shape
    features = proj.shape[1]
    pad = router.shape[1]
    tile = min(ROWS, count)

    def rows(extent):
        return pl.BlockSpec((tile, extent), lambda i, w: (i, 0))

    def whole(array):
        return pl.BlockSpec(array.shape, lambda i, w: (0,) * array.ndim)

    return pl.pallas_call(
        functools.partial(home_kernel, limit),
        name="home_step",
        out_shape=(
            shape_of((count, width), BF16),
            shape_of((count, width), F32),
            shape_of((count, width), BF16),
            shape_of((ctxs, count, features // ctxs), BF16),
            shape_of((count, pad), BF16),
            shape_of((1, width), F32),
        ),
        grid_spec=pltpu.PrefetchScalarGridSpec(
            num_scalar_prefetch=1,
            grid=(count // tile,),
            in_specs=[
                rows(width), rows(width), rows(width), rows(pad), rows(1), rows(1), rows(1),
                whole(own_slot), whole(par_slot), whole(back_own), whole(back_par), whole(grads),
                whole(gain), whole(router), whole(proj),
            ],
            out_specs=[
                rows(width), rows(width), rows(width),
                pl.BlockSpec((ctxs, tile, features // ctxs), lambda i, w: (0, i, 0)), rows(pad),
                pl.BlockSpec((1, width), lambda i, w: (0, 0)),
            ],
        ),
    )(
        where, cot, middle, second, probs, gate, route, target, own_slot, par_slot, back_own, back_par,
        grads, gain, router, proj,
    )


def last_kernel(tokens_ref, grad_middle_ref, own_ref, par_ref, weight_own_ref, weight_par_ref, out_ref):
    ctxs, _, piece = own_ref.shape
    scaled = None
    for got, weight in ((own_ref, weight_own_ref), (par_ref, weight_par_ref)):
        for c in range(ctxs):
            part = nt(got[c], weight[:, c * piece : (c + 1) * piece])
            scaled = part if scaled is None else scaled + part
    unit, inverse = normed(tokens_ref[...].astype(F32))
    out_ref[...] = grad_middle_ref[...] + norm_back(scaled, unit, inverse)


def last_step(tokens, grad_middle, own, par, weight_own, weight_par):
    count, width = tokens.shape
    ctxs, _, piece = own.shape
    tile = min(ROWS, count)
    rows = pl.BlockSpec((tile, width), lambda i: (i, 0))
    got = pl.BlockSpec((ctxs, tile, piece), lambda i: (0, i, 0))
    weight = pl.BlockSpec(weight_own.shape, lambda i: (0, 0))
    return pl.pallas_call(
        last_kernel,
        name="last_step",
        grid=(count // tile,),
        out_shape=shape_of((count, width), F32),
        in_specs=[rows, rows, got, got, weight, weight],
        out_specs=rows,
    )(tokens, grad_middle, own, par, weight_own, weight_par)


def expert_forward_kernel(rows_ref, w_in_ref, w_out_ref, hidden_ref, slope_ref, out_ref, total):
    j = pl.program_id(0)
    pre = nn(rows_ref[...], w_in_ref[...])
    square = pre * pre
    bend = jnp.tanh(pre * (GELU_A + (GELU_A * GELU_B) * square))
    rise = 0.5 + 0.5 * bend
    hidden = (pre * rise).astype(BF16)
    hidden_ref[...] = hidden
    slope = rise + (0.5 * pre) * (1.0 - bend * bend) * (GELU_A + (3.0 * GELU_A * GELU_B) * square)
    slope_ref[...] = slope.astype(BF16)
    part = nn(hidden, w_out_ref[...])

    @pl.when(j == 0)
    def _():
        total[...] = part

    @pl.when(j > 0)
    def _():
        total[...] += part

    @pl.when(j == pl.num_programs(0) - 1)
    def _():
        out_ref[...] = total[...].astype(BF16)


def expert_backward_kernel(grad_ref, slope_ref, w_in_ref, w_out_ref, grad_pre_ref, out_ref, total):
    j = pl.program_id(0)
    grad_pre = (nt(grad_ref[...], w_out_ref[...]) * slope_ref[...].astype(F32)).astype(BF16)
    grad_pre_ref[...] = grad_pre
    part = nt(grad_pre, w_in_ref[...])

    @pl.when(j == 0)
    def _():
        total[...] = part

    @pl.when(j > 0)
    def _():
        total[...] += part

    @pl.when(j == pl.num_programs(0) - 1)
    def _():
        out_ref[...] = total[...].astype(BF16)


UNITS = 256


def expert_step(kernel, operands, w_in, w_out, results):
    width, units = w_in.shape
    count = operands[0].shape[0]
    tile = min(UNITS, units)
    whole = pl.BlockSpec((count, width), lambda j: (0, 0))
    part = pl.BlockSpec((count, tile), lambda j: (0, j))
    return pl.pallas_call(
        kernel,
        grid=(units // tile,),
        out_shape=(shape_of((count, units), BF16),) * results + (shape_of((count, width), BF16),),
        in_specs=[whole] + [part] * (len(operands) - 1)
        + [pl.BlockSpec((width, tile), lambda j: (0, j)), pl.BlockSpec((tile, width), lambda j: (j, 0))],
        out_specs=(part,) * results + (whole,),
        scratch_shapes=[pltpu.VMEM((count, width), F32)],
    )(*operands, w_in, w_out)


def owner_kernel(shards, ctxs, wide, got_ref, weight_ref, gain_ref, grad_ref, sum_ref):
    gain = gain_ref[...].astype(F32)
    total = jnp.zeros((got_ref.shape[1], 1), F32)
    for c in range(ctxs):
        raw = got_ref[c].astype(F32)
        for s in range(1, shards):
            raw = raw + got_ref[s * ctxs + c].astype(F32)
        for k in range(3):
            piece = raw[:, k * wide : (k + 1) * wide]
            grad_ref[k, :, c * wide : (c + 1) * wide] = piece * gain
            weight = weight_ref[k, :, c * wide : (c + 1) * wide].astype(F32)
            total = total + jnp.sum(piece * weight, axis=-1, keepdims=True)
    sum_ref[...] = jnp.broadcast_to(total, sum_ref.shape)


def owner_step(got, weight_qkv, gain, shards, ctxs, wide):
    rows = weight_qkv.shape[1]
    return pl.pallas_call(
        functools.partial(owner_kernel, shards, ctxs, wide),
        name="owner_step",
        out_shape=(shape_of(weight_qkv.shape, F32), shape_of((rows, 128), F32)),
        in_specs=[pl.BlockSpec(memory_space=pltpu.VMEM)] * 3,
        out_specs=(pl.BlockSpec(memory_space=pltpu.VMEM),) * 2,
    )(got, weight_qkv, gain)


def local(
    sizes, tokens, lengths, routes, weight_qkv, weight_proj, router, gain_one, gain_two,
    w_in, w_out, cotangent,
):
    shards, ctxs, tps = sizes
    group = ("shard", "ctx")
    groups = shards * ctxs
    slots, count, width = tokens.shape
    assert slots == 1 and tps == 2
    head_width = weight_qkv.shape[2]
    wide = head_width // ctxs
    heads = wide // HEAD_DIM
    rows = weight_qkv.shape[1]
    experts = router.shape[1]
    capacity = max(2, (5 * count + 4 * experts - 1) // (4 * experts))
    assert capacity % 2 == 0
    half_cap = capacity // 2
    half = count // tps
    length_all = ctxs * count
    ctx_rank = lax.axis_index("ctx")
    tp_rank = lax.axis_index("tp")
    rows_in = tokens[0]
    cot = cotangent[0]

    pad = -(-(experts + 2) // 128) * 128
    small = jnp.concatenate(
        [router, gain_two[:, None], gain_one[:, None], jnp.zeros((rows, pad - experts - 2), BF16)],
        axis=1,
    )
    unit_half, sent_weights, row_weights = prepare(
        rows_in, weight_qkv, small, tp_rank.astype(jnp.int32)[None], half, ctxs, wide, experts
    )
    unit_all, got_weights = gather_step(1, sizes, unit_half, sent_weights)
    unit_all, got_weights, row_weights, weight_late, routes, cot_late = lax.optimization_barrier(
        (unit_all, got_weights, row_weights, weight_proj, routes, cot)
    )
    whole_qkv = lax.all_gather(row_weights, group, axis=0, tiled=True)
    whole_proj = lax.all_gather(weight_late, group, axis=0, tiled=True)
    unit_all = unit_all.reshape(length_all, width)
    got_weights = got_weights.reshape(width, 3 * wide + pad)
    own_qkv = got_weights[:, : 3 * wide]
    full_small = got_weights[:, 3 * wide :]
    full_two = got_weights[:, 3 * wide + experts].reshape(1, width)

    places = ctx_rank * count + jnp.arange(count, dtype=jnp.int32)
    route = routes.reshape(count)
    valid = places < lengths[0]
    route_hot = route[:, None] == jnp.arange(experts, dtype=jnp.int32)[None, :]
    counted = (route_hot & valid[:, None]).astype(BF16)
    order = jnp.arange(count, dtype=jnp.int32)
    below = (order[:, None] > order[None, :]).astype(BF16)
    earlier = nn(below, counted)
    place = jnp.sum(earlier * counted.astype(F32), axis=1).astype(jnp.int32)
    kept = valid & (place < capacity)
    target = jnp.where(kept, route * capacity + place, experts * capacity)
    slot = jnp.arange(experts * half_cap, dtype=jnp.int32)
    slot = (slot // half_cap) * capacity + slot % half_cap
    own_slot = slot + tp_rank * half_cap
    par_slot = slot + (1 - tp_rank) * half_cap
    picked = own_slot[:, None] == target[None, :]
    pick_own = picked.astype(BF16)

    sent_cot = nn(pick_own, cot_late).astype(BF16).reshape(experts, half_cap, width)
    got_cot = lax.all_to_all(sent_cot, group, split_axis=0, concat_axis=0, tiled=True)

    projected = nn(unit_all, own_qkv).astype(BF16)
    mixed_heads, lse = attention_forward(projected, lengths, heads)

    def passed(array):
        return Item(
            "pair", array, [shape_of(array.shape, BF16)],
            lambda ref, p: ref, None, relay=lambda ref, q, t: ref, keep=False,
        )

    mixed_own, mixed_par, proj_par = exchange(
        2, sizes,
        [
            Item(
                "ctx", mixed_heads,
                [shape_of((count, head_width), BF16), shape_of((count, head_width), BF16)],
                lambda ref, p: ref.at[pl.ds(pl.multiple_of(p * count, count), count), :],
                lambda ref, q, t: ref.at[:, pl.ds(pl.multiple_of(q * wide, wide), wide)],
                relay=lambda ref, q, t: ref.at[:, pl.ds(pl.multiple_of(q * wide, wide), wide)],
                block=(count, wide),
            ),
            passed(whole_proj),
        ],
    )

    route_column = routes.reshape(count, 1)
    middle, second, probs, gate = middle_step(
        rows_in, mixed_own, mixed_par, whole_proj, proj_par, full_two, full_small, route_column, experts
    )
    sent_rows = nn(pick_own, second).astype(BF16).reshape(experts, half_cap, width)
    gate_rows = jnp.sum(jnp.where(picked, gate.reshape(1, count), 0.0), axis=1)
    gate_rows = gate_rows.reshape(experts, half_cap)
    lanes = -(-half_cap // 128) * 128
    gate_rows = jnp.broadcast_to(
        jnp.pad(gate_rows, ((0, 0), (0, lanes - half_cap)))[:, None, :], (experts, 8, lanes)
    )

    def scattered(array):
        block = array.shape[1:]
        return Item(
            "all", array, [shape_of((tps,) + array.shape, array.dtype)],
            lambda ref, p: ref.at[p],
            lambda ref, q, t: ref.at[0, q],
            relay=lambda ref, q, t: ref.at[1, q],
            block=block,
        )

    got_gates, got_rows, cot_par = exchange(
        3, sizes, [scattered(gate_rows), scattered(sent_rows), passed(got_cot)]
    )

    slots_half = groups * half_cap
    total_rows = tps * slots_half
    arrived = got_rows.reshape(total_rows, width)
    gates = got_gates[:, :, 0, :half_cap].reshape(total_rows)
    cot_rows = jnp.concatenate([got_cot, cot_par], axis=0).reshape(total_rows, width)
    grad_rows = (gates[:, None] * cot_rows.astype(F32)).astype(BF16)
    hidden, slope, partial_out = expert_step(
        expert_forward_kernel, (arrived,), w_in[0], w_out[0], 2
    )
    summed = pair_sum(4, partial_out.reshape(tps, groups, half_cap, width))
    going_back = lax.all_to_all(summed, group, split_axis=0, concat_axis=0, tiled=True)

    grad_pre, partial_grad = expert_step(
        expert_backward_kernel, (grad_rows, slope), w_in[0], w_out[0], 1
    )
    grad_summed = pair_sum(5, partial_grad.reshape(tps, groups, half_cap, width))
    grad_home, back_par, qkv_par = exchange(
        6, sizes, [scattered(grad_summed), passed(going_back), passed(whole_qkv)]
    )

    where = jnp.stack([ctx_rank * count, lengths[0]]).astype(jnp.int32)
    output, grad_middle, grad_branch, grad_mixed_own, grad_logits, grad_gain_two = home_step(
        cot, middle, second, probs, gate, route_column, target.reshape(count, 1),
        own_slot.reshape(1, slots_half), par_slot.reshape(1, slots_half),
        going_back.reshape(slots_half, width), back_par.reshape(slots_half, width),
        grad_home.reshape(tps, slots_half, width), full_two, full_small, whole_proj, where,
        experts * capacity, ctxs,
    )
    output = output.reshape(slots, count, width)

    (grad_mixed,) = exchange(
        7, sizes,
        [
            Item(
                "ctx", grad_mixed_own, [shape_of((length_all, wide), BF16)],
                lambda ref, p: ref.at[p],
                lambda ref, q, t: ref.at[pl.ds(pl.multiple_of(q * count, count), count), :],
                block=(count, wide),
            ),
        ],
    )
    grad_router = tn(second, grad_logits)[:, :experts]
    grad_proj = tn(grad_branch, mixed_own)
    packed = jnp.concatenate(
        [
            grad_proj, grad_router, grad_gain_two.reshape(width, 1),
            jnp.zeros((width, pad - experts - 1), F32),
        ],
        axis=1,
    )
    owned = lax.psum_scatter(packed, group, scatter_dimension=0, tiled=True)
    owned_proj = owned[:, :head_width]
    owned_router = owned[:, head_width : head_width + experts]
    owned_two = owned[:, head_width + experts]

    grad_projected = attention_backward(projected, mixed_heads, grad_mixed, lse, lengths, heads)
    grad_own = lax.all_to_all(
        grad_projected.reshape(ctxs, count, 3 * wide), "ctx", split_axis=0, concat_axis=0, tiled=True
    )

    unit_late, hidden, arrived, grad_rows, grad_pre, grad_projected = lax.optimization_barrier(
        (unit_all, hidden, arrived, grad_rows, grad_pre, grad_projected)
    )
    grad_weight = tn(unit_late, grad_projected).astype(BF16).reshape(groups, rows, 3 * wide)
    grad_w_out = tn(hidden, grad_rows)[None]
    grad_w_in = tn(arrived, grad_pre)[None]
    grad_weight, grad_own = lax.optimization_barrier((grad_weight, grad_own))
    got_grad = lax.all_to_all(grad_weight, group, split_axis=0, concat_axis=0, tiled=True)

    (grad_par,) = exchange(8, sizes, [passed(grad_own)])
    grad_tokens = last_step(rows_in, grad_middle, grad_own, grad_par, whole_qkv, qkv_par)
    grad_tokens = grad_tokens.reshape(slots, count, width)
    owned_qkv, sums = owner_step(got_grad, weight_qkv, gain_one.reshape(rows, 1), shards, ctxs, wide)
    owned_one = lax.psum(sums[:, 0], "tp")
    return (
        output,
        grad_tokens,
        owned_qkv,
        owned_proj,
        owned_router,
        owned_one,
        owned_two,
        grad_w_in,
        grad_w_out,
    )


def solution(mesh):
    sizes = (mesh.shape["shard"], mesh.shape["ctx"], mesh.shape["tp"])
    return jax.shard_map(
        functools.partial(local, sizes),
        mesh=mesh,
        in_specs=(
            P("shard", "ctx", None),
            P("shard"),
            P("shard", "ctx", None),
            P(None, ("shard", "ctx"), "tp"),
            P(("shard", "ctx"), "tp"),
            P(("shard", "ctx"), None),
            P(("shard", "ctx")),
            P(("shard", "ctx")),
            P(("shard", "ctx"), None, "tp"),
            P(("shard", "ctx"), "tp", None),
            P("shard", "ctx", None),
        ),
        out_specs=(
            P("shard", "ctx", None),
            P("shard", "ctx", None),
            P(None, ("shard", "ctx"), "tp"),
            P(("shard", "ctx"), "tp"),
            P(("shard", "ctx"), None),
            P(("shard", "ctx")),
            P(("shard", "ctx")),
            P(("shard", "ctx"), None, "tp"),
            P(("shard", "ctx"), "tp", None),
        ),
        check_vma=False,
    )
```
